32 devices in a mesh: bx: 4 (over y, core), by: 8 (over z, x).
Axes of the slice: x: 2, y: 2, z: 4, core: 2. Of those that a mesh axis runs over, the one named last changes fastest.
Arguments:
- h_old: float32 [20, 256, 1024], P(None, 'bx', 'by'), may hold values from -3 to 0.5
- soil_type: int32 [20, 256, 1024], P(None, 'bx', 'by'), may hold values from 0 to 11
- ks_scale: float32 [20, 256, 1024], P(None, 'bx', 'by'), may hold values from 0.3 to 3
- soil_table: float32 [4, 12], replicated, may hold values from 0.2 to 1
- clump_brick: int32 [262144], P(('bx', 'by')), may hold values from -1 to 31, as said below
- clump_cell: int32 [262144], P(('bx', 'by')), may hold values from -1 to 8191, as said below
- root_fraction: float32 [14, 262144], P(None, ('bx', 'by')), may hold values from 0.05 to 0.3
- transpiration: float32 [262144], P(('bx', 'by')), may hold values from 0.2 to 2
- infiltration: float32 [262144], P(('bx', 'by')), may hold values from 0.2 to 2
Outputs:
- pressure: float32 [20, 256, 1024], P(None, 'bx', 'by')
- stress: float32 [262144], P(('bx', 'by'))
The draws below stay inside these ranges and needn't reach their ends.
Inputs may be any that keep to these rules, and one draw needn't show every extreme that they name: `clump_brick`: A brick is the 64 x 128 columns with i // 64 and j // 128 fixed, numbered (i // 64) * 8 + j // 128. The slots of one device are the 8192 consecutive entries of its shard; its slots b * 256 to (b + 1) * 256 - 1 hold columns of brick b or are empty, and there the entry is b; -1 marks an empty slot (exactly where clump_cell is -1). `clump_cell`: A slot's entry is the position (i % 64) * 128 + j % 128 of its column within its brick, or -1 when empty; no column is held twice. In every draw one brick has all its columns held, all 256 of its slots filled on every device.
All inputs are finite; a program needn't handle non-finite values.
Results may differ from the reference program's by a relative error of at most 0.000068.
Values sent between devices are 32-bit elements; how exact they have to be, the bound alone decides.
No kernel may reach another device: no remote copies, remote signals or barrier semaphores. Data moves between devices by JAX's collectives and lax.ppermute only.
A program may use at most 64 MiB of HBM per device.

```python
import math
import jax
import jax.numpy as jnp
from jax import lax

CX = 64
CY = 128
LAY = 20
ROOT = 14
ITERS = 2
NSOIL = 12
NXG = 256
NYG = 1024
COLUMNS = 262144
N_BX = 4
N_BY = 8


def clump_layout(key):
    devices = N_BX * N_BY
    per_device = CX * CY
    per_peer = per_device // devices
    keys = jax.random.split(key, 5)
    levels = jax.random.randint(keys[0], (devices,), per_peer // 2 + 1, per_peer + 1)
    counts = jax.random.randint(keys[1], (devices, devices), 0, levels[None, :] + 1)
    busiest = jax.random.randint(keys[2], (), 0, devices)
    brick_ids = jnp.arange(devices, dtype=jnp.int32)
    counts = jnp.where(brick_ids[None, :] == busiest, per_peer, counts).astype(jnp.int32)
    offsets = jnp.cumsum(counts, axis=0) - counts
    spread = max(2, 2 ** 30 // per_device)
    scores = jax.random.randint(keys[3], (devices, per_device), 0, spread) * per_device + jnp.arange(per_device, dtype=jnp.int32)[None, :]
    perms = jnp.argsort(scores, axis=1).astype(jnp.int32)
    within = jnp.arange(per_peer, dtype=jnp.int32)
    used = within[None, None, :] < counts[:, :, None]
    where_in = jnp.minimum(offsets[:, :, None] + within[None, None, :], per_device - 1)
    local = perms[brick_ids[None, :, None], where_in]
    brick_full = jnp.broadcast_to(brick_ids[None, :, None], local.shape)
    cell_id = jnp.where(used, local, -1)
    brick_id = jnp.where(used, brick_full, -1)
    spread_peer = max(2, 2 ** 30 // per_peer)
    shuffle = jax.random.randint(keys[4], (devices, devices, per_peer), 0, spread_peer) * per_peer + within[None, None, :]
    order = jnp.argsort(shuffle, axis=2).astype(jnp.int32)
    cells = jnp.take_along_axis(cell_id, order, axis=2).reshape(-1).astype(jnp.int32)
    bricks = jnp.take_along_axis(brick_id, order, axis=2).reshape(-1).astype(jnp.int32)
    return (bricks, cells)


def draw_clump_brick(key, part):
    bricks, cells = clump_layout(jax.random.fold_in(key, 7))
    return bricks


def draw_clump_cell(key, part):
    bricks, cells = clump_layout(jax.random.fold_in(key, 7))
    return cells


def set_ends(array, stream_key, low, top_value):
    shape = array.shape
    place = [jax.random.randint(jax.random.fold_in(stream_key, axis), (), 0, shape[axis]) for axis in range(len(shape))]
    array = array.at[tuple(place)].set(low)
    longest = shape.index(max(shape))
    place[longest] = (place[longest] + 1) % shape[longest]
    return array.at[tuple(place)].set(top_value)


def block_scale(rng, shape, pieces, low, largest):
    loudness, own = 1.0, jax.random.fold_in(rng, 6)
    for position, blocks in pieces:
        heights = jnp.exp(jax.random.uniform(jax.random.fold_in(own, position), (blocks,), jnp.float32, low / len(pieces), largest / len(pieces)))
        loudness = loudness * jnp.repeat(heights, shape[position] // blocks).reshape([-1 if axis == position else 1 for axis in range(len(shape))])
    return loudness


def setup_inputs(seed: int = 0) -> dict:
    key_list = jax.random.split(jax.random.key(seed), 10)
    h_old = jnp.clip(-3.0 + 3.5 * jax.random.uniform(key_list[0], (LAY, NXG, NYG), jnp.float32) ** block_scale(key_list[0], (LAY, NXG, NYG), ((1, 4), (2, 8)), -0.2, 0.2), -3.0, 0.5)
    soil_type = set_ends(jax.random.randint(key_list[1], (LAY, NXG, NYG), 0, NSOIL), jax.random.fold_in(key_list[1], 1), 0, NSOIL - 1).astype(jnp.int32)
    ks_scale = jnp.clip(jnp.exp(math.log(3.0) - 2.3025851 * jax.random.uniform(key_list[2], (LAY, NXG, NYG), jnp.float32) ** block_scale(key_list[2], (LAY, NXG, NYG), ((1, 4), (2, 8)), -0.2, 0.2)), 0.3, 3.0)
    soil_table = jnp.clip(jax.random.uniform(key_list[3], (4, NSOIL), jnp.float32, 0.2, 1.0), 0.2, 1.0)
    clump_brick = draw_clump_brick(jax.random.fold_in(key_list[9], 71), 0)
    clump_cell = draw_clump_cell(jax.random.fold_in(key_list[9], 71), 0)
    root_fraction = jnp.clip(0.05 + 0.25 * jax.random.uniform(key_list[6], (ROOT, COLUMNS), jnp.float32) ** block_scale(key_list[6], (ROOT, COLUMNS), ((1, 32),), -0.2, 0.2), 0.05, 0.3)
    transpiration = jnp.clip(jnp.exp(math.log(2.0) - 2.3025851 * jax.random.uniform(key_list[7], (COLUMNS,), jnp.float32) ** block_scale(key_list[7], (COLUMNS,), ((0, 32),), -0.2, 0.2)), 0.2, 2.0)
    infiltration = jnp.clip(jnp.exp(math.log(2.0) - 2.3025851 * jax.random.uniform(key_list[8], (COLUMNS,), jnp.float32) ** block_scale(key_list[8], (COLUMNS,), ((0, 32),), -0.2, 0.2)), 0.2, 2.0)
    return {"h_old": h_old, "soil_type": soil_type, "ks_scale": ks_scale, "soil_table": soil_table, "clump_brick": clump_brick, "clump_cell": clump_cell, "root_fraction": root_fraction, "transpiration": transpiration, "infiltration": infiltration}


RESIDUAL_WATER = 0.05
STORAGE = 0.2
TIME_STEP = 0.5
LATERAL = 0.5

def closures(pressure, scale_alpha, shape_n, porosity, ksat):
    exponent = 1.0 - 1.0 / shape_n
    suction = scale_alpha * jnp.maximum(-pressure, 0.0)
    base_term = 1.0 + jnp.power(suction, shape_n)
    saturation = jnp.power(base_term, -exponent)
    moisture = RESIDUAL_WATER + (porosity - RESIDUAL_WATER) * saturation
    inner_term = 1.0 - jnp.power(1.0 - jnp.power(saturation, 1.0 / exponent), exponent)
    conduct = ksat * jnp.sqrt(saturation) * inner_term * inner_term
    storage = STORAGE + (porosity - RESIDUAL_WATER) * exponent * shape_n * scale_alpha * jnp.power(suction, shape_n - 1.0) * jnp.power(base_term, -exponent - 1.0)
    return (saturation, moisture, conduct, storage)

def thomas(diagonal, coupling, target):
    layers = diagonal.shape[0]
    ratios = []
    values = []
    pivot_value = diagonal[0]
    if layers > 1:
        ratios.append(coupling[0] / pivot_value)
    values.append(target[0] / pivot_value)
    for layer_index in range(1, layers):
        pivot_value = diagonal[layer_index] - coupling[layer_index - 1] * ratios[layer_index - 1]
        if layer_index < layers - 1:
            ratios.append(coupling[layer_index] / pivot_value)
        values.append((target[layer_index] - coupling[layer_index - 1] * values[layer_index - 1]) / pivot_value)
    result = [values[layers - 1]]
    for layer_index in range(layers - 2, -1, -1):
        result.insert(0, values[layer_index] - ratios[layer_index] * result[0])
    return jnp.stack(result)

def reference(h_old, soil_type, ks_scale, soil_table, clump_brick, clump_cell, root_fraction, transpiration, infiltration):
    params = jnp.take(soil_table, soil_type, axis=1)
    scale_alpha = 4.0 * params[0]
    shape_n = 1.2 + 2.0 * params[1]
    ksat = 3.0 * params[2] * ks_scale
    porosity = 0.3 + 0.3 * params[3]
    columns = NXG * NYG
    valid = clump_cell >= 0
    brick_safe = jnp.where(valid, clump_brick, 0).astype(jnp.int32)
    cell_safe = jnp.where(valid, clump_cell, 0).astype(jnp.int32)
    row_global = brick_safe // N_BY * CX + cell_safe // CY
    col_global = brick_safe % N_BY * CY + cell_safe % CY
    column_id = (row_global * NYG + col_global).astype(jnp.int32)
    target_index = jnp.where(valid, column_id, columns).astype(jnp.int32)
    forcing = jnp.concatenate([root_fraction, transpiration[None], infiltration[None]], 0)
    grid = jnp.zeros((ROOT + 2, columns), jnp.float32).at[:, target_index].set(forcing, mode='drop')
    grid = grid.reshape(ROOT + 2, NXG, NYG)
    sink = grid[ROOT][None] * grid[:ROOT]
    sink_full = jnp.concatenate([sink, jnp.zeros((LAY - ROOT, NXG, NYG), jnp.float32)], 0)
    inflow_top = grid[ROOT + 1]
    pressure = h_old
    saturation, moisture, conduct, storage = closures(pressure, scale_alpha, shape_n, porosity, ksat)
    moisture_old = moisture
    for step_index in range(ITERS):
        vert_k = 0.5 * (conduct[:-1] + conduct[1:])
        vert_flux = vert_k * (pressure[:-1] - pressure[1:] + 1.0)
        down_out = jnp.concatenate([vert_flux, conduct[-1:]], 0)
        from_above = jnp.concatenate([inflow_top[None], vert_flux], 0)
        face_x = 0.5 * (conduct[:, :-1] + conduct[:, 1:])
        flow_x = LATERAL * face_x * (pressure[:, :-1] - pressure[:, 1:])
        face_y = 0.5 * (conduct[:, :, :-1] + conduct[:, :, 1:])
        flow_y = LATERAL * face_y * (pressure[:, :, :-1] - pressure[:, :, 1:])
        pad_hi_x = ((0, 0), (0, 1), (0, 0))
        pad_lo_x = ((0, 0), (1, 0), (0, 0))
        pad_hi_y = ((0, 0), (0, 0), (0, 1))
        pad_lo_y = ((0, 0), (0, 0), (1, 0))
        lateral = jnp.pad(flow_x, pad_hi_x) - jnp.pad(flow_x, pad_lo_x) + (jnp.pad(flow_y, pad_hi_y) - jnp.pad(flow_y, pad_lo_y))
        residual = (moisture - moisture_old) / TIME_STEP + (down_out - from_above) + lateral + sink_full
        lateral_sum = jnp.pad(face_x, pad_hi_x) + jnp.pad(face_x, pad_lo_x) + (jnp.pad(face_y, pad_hi_y) + jnp.pad(face_y, pad_lo_y))
        diagonal = storage / TIME_STEP + jnp.pad(vert_k, ((1, 0), (0, 0), (0, 0))) + jnp.pad(vert_k, ((0, 1), (0, 0), (0, 0))) + LATERAL * lateral_sum
        delta = thomas(diagonal, -vert_k, -residual)
        pressure = pressure + delta
        saturation, moisture, conduct, storage = closures(pressure, scale_alpha, shape_n, porosity, ksat)
    root_state = saturation[:ROOT].reshape(ROOT, columns)
    safe_col = jnp.where(valid, column_id, 0).astype(jnp.int32)
    at_slot = root_state[:, safe_col]
    numer = lax.optimization_barrier(jnp.sum(root_fraction * at_slot, 0))
    denom = lax.optimization_barrier(jnp.sum(root_fraction, 0))
    stress = jnp.where(valid, numer / denom, 0.0)
    return (pressure, stress)
```

```python
import jax
import jax.numpy as jnp
from jax import lax
from jax.experimental import pallas as pl
from jax.experimental.pallas import tpu as pltpu
from jax.sharding import PartitionSpec as P

ITERS = 2
RESIDUAL_WATER = 0.05
STORAGE = 0.2
TIME_STEP = 0.5
LATERAL = 0.5
TINY = 1e-30
ROW_BLOCK = 32
PAD = 8
F32 = jnp.float32
BF16 = jnp.bfloat16
MIB = 1 << 20


def log2(x):
    return lax.log(x) * 1.4426950408889634


def lane_table(table, layers_like):
    t0, t1, t2, t3 = (table[i : i + 1, :] for i in range(4))
    alpha = 4.0 * t0
    n1 = 0.2 + 2.0 * t1
    half_m = 0.5 * n1 / (1.0 + n1)
    ks3 = 3.0 * t2
    room = (0.3 - RESIDUAL_WATER) + 0.3 * t3
    return [jnp.broadcast_to(r, layers_like) for r in (alpha, n1, half_m, ks3, room)]


def closure(head, alpha, n1, half_m, ksat, cap):
    suction = jnp.maximum(alpha * jnp.maximum(-head, 0.0), TINY)
    power = jnp.exp2(n1 * log2(suction))
    log_base = log2(1.0 + suction * power)
    root = jnp.exp2(-(half_m * log_base))
    saturation = root * root
    share = power * saturation
    inner = 1.0 - share
    conduct = ksat * root * (inner * inner)
    storage = STORAGE / TIME_STEP + cap * (share * jnp.exp2(-log_base))
    return saturation, conduct, storage


def lane_lookup(row, index):
    return jnp.take_along_axis(row, index, axis=1, mode="promise_in_bounds")


def edge_messages(head, conduct, k, lanes, packed):
    width = lanes.shape[1]
    for base, value in ((0, head), (width // 2, conduct)):
        moved = pltpu.roll(value, base + 2 * k + 1, 1)
        packed = jnp.where((lanes == base + 2 * k) | (lanes == base + 2 * k + 1), moved, packed)
    return packed


def first_kernel(
    h_ref, soil_ref, ks_ref, table_ref,
    alpha_ref, n1_ref, half_m_ref, ksat_ref, room_ref, sat_ref, cond_ref, stor_ref,
    row_even_ref, row_odd_ref, lane_ref,
):
    layers, rows, width = h_ref.shape
    tables = lane_table(table_ref[...], (rows, width))
    even = lax.rem(lax.axis_index("bx"), 2) == 0
    lanes = lax.broadcasted_iota(jnp.int32, (rows, width), 1)
    packed = jnp.zeros((rows, width), F32)
    for k in range(layers):
        head = h_ref[k]
        kind = soil_ref[k]
        alpha, n1, half_m, ks3, room = (lane_lookup(t, kind) for t in tables)
        ksat = ks3 * ks_ref[k]
        cap = (2.0 * room) * (n1 * alpha)
        saturation, conduct, storage = closure(head, alpha, n1, half_m, ksat, cap)
        alpha_ref[k] = alpha
        n1_ref[k] = n1
        half_m_ref[k] = half_m
        ksat_ref[k] = ksat
        room_ref[k] = room
        sat_ref[k] = saturation
        cond_ref[k] = conduct
        stor_ref[k] = storage
        packed = edge_messages(head, conduct, k, lanes, packed)
    lane_ref[...] = packed
    store_rows(h_ref, cond_ref, even, row_even_ref, row_odd_ref)


def store_rows(head_ref, cond_ref, even, row_even_ref, row_odd_ref):
    rows = head_ref.shape[1]
    for part, ref in enumerate((head_ref, cond_ref)):
        low = ref[:, 0, :]
        high = ref[:, rows - 1, :]
        row_even_ref[part] = jnp.where(even, high, low)
        row_odd_ref[part] = jnp.where(even, low, high)


def fill_pads(head_ref, cond_ref, row_even_ref, row_odd_ref, head_pad, cond_pad):
    rows = head_ref.shape[1]
    index = lax.axis_index("bx")
    even = lax.rem(index, 2) == 0
    first = index == 0
    last = index == lax.axis_size("bx") - 1
    for ref, pad, part, sign in ((head_ref, head_pad, 0, 1.0), (cond_ref, cond_pad, 1, -1.0)):
        pad[:, PAD : PAD + rows, :] = ref[...]
        low = jnp.where(even, row_odd_ref[part], row_even_ref[part])
        high = jnp.where(even, row_even_ref[part], row_odd_ref[part])
        pad[:, PAD - 1, :] = jnp.where(first, sign * ref[:, 0, :], low)
        pad[:, PAD + rows, :] = jnp.where(last, sign * ref[:, rows - 1, :], high)


def lane_halo(own, lane_even, lane_odd):
    index = lax.axis_index("by")
    even = lax.rem(index, 2) == 0
    width = own.shape[1]
    lanes = lax.broadcasted_iota(jnp.int32, own.shape, 1)
    sign = jnp.where(lanes < width // 2, 1.0, -1.0)
    low = jnp.where(even, lane_odd, lane_even)
    high = jnp.where(even, lane_even, lane_odd)
    low = jnp.where(index == 0, sign * pltpu.roll(own, width - 1, 1), low)
    high = jnp.where(
        index == lax.axis_size("by") - 1, sign * pltpu.roll(own, 1, 1), high
    )
    return jnp.where(lax.rem(lanes, 2) == 0, low, pltpu.roll(high, width - 2, 1))


def lateral_terms(k, head_pad, cond_pad, halo, lanes):
    rows = head_pad.shape[1] - 2 * PAD
    width = head_pad.shape[2]
    at = lambda pad, move: pad[k, PAD + move : PAD + move + rows, :]
    head, conduct = at(head_pad, 0), at(cond_pad, 0)
    halo_head = pltpu.roll(halo, (width - 2 * k) % width, 1)
    halo_cond = pltpu.roll(halo, (width // 2 - 2 * k) % width, 1)
    first = lanes == 0
    last = lanes == width - 1
    pairs = [
        (at(head_pad, -1), at(cond_pad, -1)),
        (at(head_pad, 1), at(cond_pad, 1)),
        (
            jnp.where(first, halo_head, pltpu.roll(head, 1, 1)),
            jnp.where(first, halo_cond, pltpu.roll(conduct, 1, 1)),
        ),
        (
            jnp.where(last, halo_head, pltpu.roll(head, width - 1, 1)),
            jnp.where(last, halo_cond, pltpu.roll(conduct, width - 1, 1)),
        ),
    ]
    flow = 0.0
    faces = 0.0
    for other_head, other_cond in pairs:
        both = conduct + other_cond
        flow = flow + both * (head - other_head)
        faces = faces + both
    return head, conduct, (0.5 * LATERAL) * flow, (0.5 * LATERAL) * faces


def factor_kernel(
    h_ref, cond_ref, stor_ref, row_even_ref, row_odd_ref, own_ref, lane_even_ref, lane_odd_ref,
    res_ref, inv_ref, vert_ref,
    head_pad, cond_pad,
):
    layers, rows, width = h_ref.shape
    fill_pads(h_ref, cond_ref, row_even_ref, row_odd_ref, head_pad, cond_pad)
    halo = lane_halo(own_ref[...], lane_even_ref[...], lane_odd_ref[...])
    lanes = lax.broadcasted_iota(jnp.int32, (rows, width), 1)
    vert_above = flux_above = ratio_above = None
    for k in range(layers):
        head, conduct, flow, faces = lateral_terms(k, head_pad, cond_pad, halo, lanes)
        diagonal = stor_ref[k] + faces
        if k < layers - 1:
            vert = 0.5 * (conduct + cond_ref[k + 1])
            flux = vert * (head - h_ref[k + 1] + 1.0)
            diagonal = diagonal + vert
        else:
            vert = None
            flux = conduct
        residual = flux + flow
        if k:
            residual = residual - flux_above
            diagonal = diagonal + vert_above
            diagonal = diagonal - vert_above * ratio_above
        inverse = 1.0 / diagonal
        res_ref[k] = residual
        inv_ref[k] = inverse
        if vert is not None:
            vert_ref[k] = vert
            ratio_above = vert * inverse
        vert_above, flux_above = vert, flux


def solve(residuals, inverses, verts):
    layers = len(residuals)
    values = []
    for k in range(layers):
        target = -residuals[k]
        if k:
            target = target + verts[k - 1]() * values[k - 1]
        values.append(target * inverses[k]())
    result = [values[layers - 1]]
    for k in range(layers - 2, -1, -1):
        result.insert(0, values[k] + (verts[k]() * inverses[k]()) * result[0])
    return result


def slot_places(ids, width):
    shift = width.bit_length() - 1
    row = ids >> shift
    return row & (ROW_BLOCK - 1), (row // ROW_BLOCK) * width + (ids & (width - 1))


def one_hot(ids, count, dtype):
    place = lax.broadcasted_iota(jnp.int32, (count, ids.shape[1]), 0)
    return (place == ids).astype(dtype)


def middle_kernel(
    slots_ref, h_ref, res_ref, inv_ref, vert_ref,
    alpha_ref, n1_ref, half_m_ref, ksat_ref, room_ref,
    head_ref, sat_ref, cond_ref, stor_ref, sink_ref, row_even_ref, row_odd_ref, lane_ref,
    total, left,
):
    layers, rows, width = h_ref.shape
    peers, fields, per_peer = slots_ref.shape
    roots = fields - 2
    values = fields - 1
    blocks = rows // ROW_BLOCK
    half = values * ROW_BLOCK
    total[...] = jnp.zeros_like(total)

    def place(peer, carry):
        block = slots_ref[peer]
        row, column = slot_places(block[values : values + 1, :].astype(jnp.int32), width)
        hot = one_hot(column, blocks * width, F32).astype(BF16)
        mask = lax.broadcasted_iota(jnp.int32, (ROW_BLOCK, per_peer), 0) == row
        high = block.astype(BF16).astype(F32)
        low = block - high
        for f in range(values):
            at = f * ROW_BLOCK
            left[at : at + ROW_BLOCK, :] = jnp.where(mask, high[f : f + 1, :], 0.0).astype(BF16)
            at = at + half
            left[at : at + ROW_BLOCK, :] = jnp.where(mask, low[f : f + 1, :], 0.0).astype(BF16)
        total[...] += lax.dot_general(
            left[...], hot, (((1,), (1,)), ((), ())), preferred_element_type=F32
        )
        return carry

    lax.fori_loop(0, peers, place, 0)

    def grid(f):
        at = f * ROW_BLOCK
        pieces = [
            total[at : at + ROW_BLOCK, b * width : (b + 1) * width]
            + total[half + at : half + at + ROW_BLOCK, b * width : (b + 1) * width]
            for b in range(blocks)
        ]
        return jnp.concatenate(pieces, 0)

    residuals = []
    for k in range(layers):
        residual = res_ref[k]
        if k < roots:
            sink = grid(k)
            sink_ref[k] = sink
            residual = residual + sink
        if k == 0:
            residual = residual - grid(roots)
        residuals.append(residual)
    sink_ref[roots] = grid(roots)
    inverses = [lambda k=k: inv_ref[k] for k in range(layers)]
    verts = [lambda k=k: vert_ref[k] for k in range(layers - 1)]
    delta = solve(residuals, inverses, verts)
    even = lax.rem(lax.axis_index("bx"), 2) == 0
    lanes = lax.broadcasted_iota(jnp.int32, (rows, width), 1)
    packed = jnp.zeros((rows, width), F32)
    for k in range(layers):
        head_ref[k] = h_ref[k] + delta[k]
    for k in range(layers):
        head = head_ref[k]
        alpha, n1 = alpha_ref[k], n1_ref[k]
        cap = (2.0 * room_ref[k]) * (n1 * alpha)
        saturation, conduct, storage = closure(
            head, alpha, n1, half_m_ref[k], ksat_ref[k], cap
        )
        sat_ref[k] = saturation
        cond_ref[k] = conduct
        stor_ref[k] = storage
        packed = edge_messages(head, conduct, k, lanes, packed)
    lane_ref[...] = packed
    store_rows(head_ref, cond_ref, even, row_even_ref, row_odd_ref)


def last_kernel(
    slots_ref, old_head_ref, old_sat_ref, sat_ref, cond_ref, stor_ref, sink_ref,
    alpha_ref, n1_ref, half_m_ref, room_ref,
    row_even_ref, row_odd_ref, own_ref, lane_even_ref, lane_odd_ref,
    head_ref, reply_ref,
    head_pad, cond_pad, inv_ref, vert_ref, value_ref,
):
    layers, rows, width = head_ref.shape
    peers, fields, per_peer = slots_ref.shape
    roots = fields - 2
    blocks = rows // ROW_BLOCK
    fill_pads(old_head_ref, cond_ref, row_even_ref, row_odd_ref, head_pad, cond_pad)
    halo = lane_halo(own_ref[...], lane_even_ref[...], lane_odd_ref[...])
    lanes = lax.broadcasted_iota(jnp.int32, (rows, width), 1)
    vert_above = flux_above = ratio_above = value = None
    for k in range(layers):
        head, conduct, flow, faces = lateral_terms(k, head_pad, cond_pad, halo, lanes)
        diagonal = stor_ref[k] + faces
        if k < layers - 1:
            vert = 0.5 * (conduct + cond_ref[k + 1])
            flux = vert * (head - old_head_ref[k + 1] + 1.0)
            diagonal = diagonal + vert
        else:
            vert = None
            flux = conduct
        residual = flux + flow + (room_ref[k] * (1.0 / TIME_STEP)) * (sat_ref[k] - old_sat_ref[k])
        if k < roots:
            residual = residual + sink_ref[k]
        if k:
            residual = residual - flux_above
            diagonal = diagonal + vert_above
            diagonal = diagonal - vert_above * ratio_above
        else:
            residual = residual - sink_ref[roots]
        inverse = 1.0 / diagonal
        target = -residual
        if k:
            target = target + vert_above * value
        value = target * inverse
        value_ref[k] = value
        if vert is not None:
            ratio_above = vert * inverse
            vert_ref[k] = ratio_above
        vert_above, flux_above = vert, flux
    change = value
    head_ref[layers - 1] = old_head_ref[layers - 1] + change
    numer = jnp.zeros((rows, width), F32)
    denom = jnp.zeros((rows, width), F32)
    for k in range(layers - 2, -1, -1):
        change = value_ref[k] + vert_ref[k] * change
        head = old_head_ref[k] + change
        head_ref[k] = head
        if k < roots:
            suction = jnp.maximum(alpha_ref[k] * jnp.maximum(-head, 0.0), TINY)
            power = jnp.exp2(n1_ref[k] * log2(suction))
            log_base = log2(1.0 + suction * power)
            saturation = jnp.exp2(-2.0 * half_m_ref[k] * log_base)
            sink = sink_ref[k]
            numer = numer + sink * saturation
            denom = denom + sink
    held = denom > 0.0
    stress = jnp.where(held, numer / jnp.where(held, denom, 1.0), 0.0)
    wide = jnp.concatenate(
        [stress[b * ROW_BLOCK : (b + 1) * ROW_BLOCK, :] for b in range(blocks)], 1
    )
    high = wide.astype(BF16)
    both = jnp.concatenate([high, (wide - high.astype(F32)).astype(BF16)], 0)

    def answer(peer, carry):
        ids = slots_ref[peer, fields - 1 : fields, :].astype(jnp.int32)
        row, column = slot_places(ids, width)
        hot = one_hot(column, blocks * width, F32).astype(BF16)
        found = jnp.dot(both, hot, preferred_element_type=F32)
        found = found[:ROW_BLOCK] + found[ROW_BLOCK:]
        mask = lax.broadcasted_iota(jnp.int32, (ROW_BLOCK, per_peer), 0) == row
        reply_ref[pl.ds(peer, 1), :] = jnp.sum(jnp.where(mask, found, 0.0), 0, keepdims=True)
        return carry

    lax.fori_loop(0, peers, answer, 0)


def swaps(size):
    even = [(i, i ^ 1) for i in range(size)]
    odd = [(i, (i + 1) % size if i % 2 else (i - 1) % size) for i in range(size)]
    return even, odd


def exchange(row_even, row_odd, packed):
    even_x, odd_x = swaps(lax.axis_size("bx"))
    even_y, odd_y = swaps(lax.axis_size("by"))
    return (
        lax.ppermute(row_even, "bx", even_x),
        lax.ppermute(row_odd, "bx", odd_x),
        packed,
        lax.ppermute(packed, "by", even_y),
        lax.ppermute(packed, "by", odd_y),
    )


def call(kernel, outs, scratch, name, limit=24):
    return pl.pallas_call(
        kernel,
        out_shape=[jax.ShapeDtypeStruct(s, F32) for s in outs],
        scratch_shapes=scratch,
        name=name,
        compiler_params=pltpu.CompilerParams(vmem_limit_bytes=limit * MIB),
    )


def on_device(
    h_old,
    soil_type,
    ks_scale,
    soil_table,
    clump_brick,
    clump_cell,
    root_fraction,
    transpiration,
    infiltration,
):
    layers, rows, width = h_old.shape
    peers = lax.axis_size("bx") * lax.axis_size("by")
    roots, slot_count = root_fraction.shape
    per_peer = slot_count // peers
    cells = (layers, rows, width)
    row_msg = (2, layers, width)
    lane_msg = (rows, width)
    axes = ("bx", "by")

    ids = jnp.where(clump_brick >= 0, clump_cell, -1).astype(F32)
    forcing = jnp.concatenate(
        [root_fraction * transpiration[None], infiltration[None], ids[None]], 0
    )
    fields = roots + 2
    slots = lax.all_to_all(
        forcing.reshape(fields, peers, per_peer).transpose(1, 0, 2),
        axes,
        split_axis=0,
        concat_axis=0,
        tiled=True,
    )
    table = jnp.pad(soil_table, ((0, 0), (0, width - soil_table.shape[1])))
    alpha, n1, half_m, ksat, room, old_sat, conduct, storage, row_even, row_odd, packed = call(
        first_kernel, [cells] * 8 + [row_msg, row_msg, lane_msg], [], "first"
    )(h_old, soil_type, ks_scale, table)
    pads = [pltpu.VMEM((layers, rows + 2 * PAD, width), F32)] * 2
    residual, inverse, vert = call(factor_kernel, [cells] * 3, pads, "factor")(
        h_old, conduct, storage, *exchange(row_even, row_odd, packed)
    )
    values = fields - 1
    blocks = rows // ROW_BLOCK
    head, sat, conduct, storage, sink, row_even, row_odd, packed = call(
        middle_kernel,
        [cells] * 4 + [(roots + 1, rows, width), row_msg, row_msg, lane_msg],
        [
            pltpu.VMEM((2 * values * ROW_BLOCK, blocks * width), F32),
            pltpu.VMEM((2 * values * ROW_BLOCK, per_peer), BF16),
        ],
        "middle",
    )(slots, h_old, residual, inverse, vert, alpha, n1, half_m, ksat, room)
    head, reply = call(
        last_kernel,
        [cells, (peers, per_peer)],
        pads + [pltpu.VMEM(cells, F32)] * 3,
        "last",
    )(
        slots, head, old_sat, sat, conduct, storage, sink, alpha, n1, half_m, room,
        *exchange(row_even, row_odd, packed),
    )
    stress = lax.all_to_all(reply, axes, split_axis=0, concat_axis=0, tiled=True)
    return head, stress.reshape(slot_count)


def solution(mesh):
    placed = (
        P(None, "bx", "by"),
        P(None, "bx", "by"),
        P(None, "bx", "by"),
        P(),
        P(("bx", "by")),
        P(("bx", "by")),
        P(None, ("bx", "by")),
        P(("bx", "by")),
        P(("bx", "by")),
    )
    return jax.shard_map(
        on_device,
        mesh=mesh,
        in_specs=placed,
        out_specs=(P(None, "bx", "by"), P(("bx", "by"))),
        check_vma=False,
    )
```

```python
import jax
import jax.numpy as jnp
from jax import lax
from jax.experimental import pallas as pl
from jax.experimental.pallas import tpu as pltpu
from jax.sharding import PartitionSpec as P

ITERS = 2
RESIDUAL_WATER = 0.05
STORAGE = 0.2
TIME_STEP = 0.5
LATERAL = 0.5
TINY = 1e-30
ROW_BLOCK = 32
HALF = 32
UNROLL = 8
GROUP = 2
LOG2E = 1.4426950408889634
PAD = 8
F32 = jnp.float32
BF16 = jnp.bfloat16
MIB = 1 << 20


def lane_tables(table, shape):
    t0, t1, t2, t3 = (table[i : i + 1, :] for i in range(4))
    alpha = 4.0 * t0
    n1 = 0.2 + 2.0 * t1
    half_m = 0.5 * n1 / (1.0 + n1)
    ks3 = (0.5 * LATERAL * 3.0) * t2
    room = ((0.3 - RESIDUAL_WATER) + 0.3 * t3) * (1.0 / TIME_STEP)
    rows = (alpha, LOG2E * n1, -LOG2E * half_m, ks3, room)
    return [jnp.broadcast_to(r, shape) for r in rows]


def powers(head, alpha, n1, half_m):
    suction = jnp.maximum(alpha * jnp.maximum(-head, 0.0), TINY)
    power = jnp.exp2(n1 * lax.log(suction))
    log_base = lax.log(1.0 + suction * power)
    return power, log_base, half_m * log_base


def closure(head, alpha, n1, half_m, ksat, room):
    power, log_base, half = powers(head, alpha, n1, half_m)
    root = jnp.exp2(half)
    saturation = root * root
    share = power * saturation
    inner = 1.0 - share
    conduct = (ksat * root) * (inner * inner)
    cap = (room * (1.0 / LOG2E)) * (n1 * alpha)
    storage = STORAGE / TIME_STEP + cap * (share * jnp.exp2(-LOG2E * log_base))
    return saturation, conduct, storage


def lane_lookup(row, index):
    return jnp.take_along_axis(row, index, axis=1, mode="promise_in_bounds")


def edge_messages(values, k, lanes, packed):
    width = lanes.shape[1]
    for part, value in enumerate(values):
        at = part * (width // 2) + 2 * k
        moved = pltpu.roll(value, at + 1, 1)
        packed = jnp.where((lanes == at) | (lanes == at + 1), moved, packed)
    return packed


def prepare_kernel(root_ref, transp_ref, infil_ref, cell_ref, out_ref):
    peers, fields, per_peer = out_ref.shape
    roots = fields - 2
    for peer in range(peers):
        at = slice(peer * per_peer, (peer + 1) * per_peer)
        out_ref[peer, :roots, :] = root_ref[:, at] * transp_ref[:, at]
        out_ref[peer, roots : roots + 1, :] = infil_ref[:, at]
        out_ref[peer, roots + 1 :, :] = cell_ref[:, at].astype(F32)


def layer_chunks(layers):
    size = 5 if layers % 5 == 0 else layers
    return [(at, size) for at in range(0, layers, size)]


def copies(pairs, sems, layers):
    chunks = layer_chunks(layers)
    return [
        [
            pltpu.make_async_copy(
                a.at[pl.ds(at, size)], b.at[pl.ds(at, size)], sems.at[c * len(pairs) + i]
            )
            for i, (a, b) in enumerate(pairs)
        ]
        for c, (at, size) in enumerate(chunks)
    ]


def first_kernel(
    h_hbm, soil_hbm, ks_hbm, table_ref,
    alpha_hbm, n1_hbm, half_m_hbm, ksat_hbm, room_hbm, sat_hbm,
    h_ref, cond_ref, stor_ref, row_even_ref, row_odd_ref, lane_ref,
    soil_ref, ks_ref, alpha_ref, n1_ref, half_m_ref, ksat_ref, room_ref, sat_ref,
    in_sems, out_sems,
):
    layers, rows, width = h_ref.shape
    ins = copies([(h_hbm, h_ref), (soil_hbm, soil_ref), (ks_hbm, ks_ref)], in_sems, layers)
    outs = copies(
        [
            (alpha_ref, alpha_hbm), (n1_ref, n1_hbm), (half_m_ref, half_m_hbm),
            (ksat_ref, ksat_hbm), (room_ref, room_hbm), (sat_ref, sat_hbm),
        ],
        out_sems,
        layers,
    )
    for chunk in ins:
        for copy in chunk:
            copy.start()
    tables = lane_tables(table_ref[...], (rows, width))
    even = lax.rem(lax.axis_index("bx"), 2) == 0
    lanes = lax.broadcasted_iota(jnp.int32, (rows, width), 1)
    packed = jnp.zeros((rows, width), F32)
    for (at, size), arrive, leave in zip(layer_chunks(layers), ins, outs):
        for copy in arrive:
            copy.wait()
        for k in range(at, at + size):
            head = h_ref[k]
            kind = soil_ref[k]
            alpha, n1, half_m, ks3, room = (lane_lookup(t, kind) for t in tables)
            ksat = ks3 * ks_ref[k]
            saturation, conduct, storage = closure(head, alpha, n1, half_m, ksat, room)
            alpha_ref[k] = alpha
            n1_ref[k] = n1
            half_m_ref[k] = half_m
            ksat_ref[k] = ksat
            room_ref[k] = room
            sat_ref[k] = saturation
            cond_ref[k] = conduct
            stor_ref[k] = storage
            packed = edge_messages((head, conduct), k, lanes, packed)
        for copy in leave:
            copy.start()
    lane_ref[...] = packed
    store_rows(h_ref, cond_ref, even, row_even_ref, row_odd_ref)
    for chunk in outs:
        for copy in chunk:
            copy.wait()


def store_rows(head_ref, cond_ref, even, row_even_ref, row_odd_ref):
    rows = head_ref.shape[1]
    for part, ref in enumerate((head_ref, cond_ref)):
        low = ref[:, 0, :]
        high = ref[:, rows - 1, :]
        row_even_ref[part] = jnp.where(even, high, low)
        row_odd_ref[part] = jnp.where(even, low, high)


def fill_pads(head_ref, cond_ref, row_even_ref, row_odd_ref, head_pad, cond_pad):
    rows = head_ref.shape[1]
    index = lax.axis_index("bx")
    even = lax.rem(index, 2) == 0
    first = index == 0
    last = index == lax.axis_size("bx") - 1
    for ref, pad, part, sign in ((head_ref, head_pad, 0, 1.0), (cond_ref, cond_pad, 1, -1.0)):
        pad[:, PAD : PAD + rows, :] = ref[...]
        low = jnp.where(even, row_odd_ref[part], row_even_ref[part])
        high = jnp.where(even, row_even_ref[part], row_odd_ref[part])
        pad[:, PAD - 1, :] = jnp.where(first, sign * ref[:, 0, :], low)
        pad[:, PAD + rows, :] = jnp.where(last, sign * ref[:, rows - 1, :], high)


def lane_halo(own, lane_even, lane_odd):
    index = lax.axis_index("by")
    even = lax.rem(index, 2) == 0
    width = own.shape[1]
    lanes = lax.broadcasted_iota(jnp.int32, own.shape, 1)
    sign = jnp.where(lanes < width // 2, 1.0, -1.0)
    low = jnp.where(even, lane_odd, lane_even)
    high = jnp.where(even, lane_even, lane_odd)
    low = jnp.where(index == 0, sign * pltpu.roll(own, width - 1, 1), low)
    high = jnp.where(
        index == lax.axis_size("by") - 1, sign * pltpu.roll(own, 1, 1), high
    )
    return jnp.where(lax.rem(lanes, 2) == 0, low, pltpu.roll(high, width - 2, 1))


def lateral_terms(k, top, size, head_pad, cond_pad, halo, lanes):
    width = head_pad.shape[2]
    at = lambda pad, move: pad[k, PAD + top + move : PAD + top + move + size, :]
    head, conduct = at(head_pad, 0), at(cond_pad, 0)
    halo_head = pltpu.roll(halo, (width - 2 * k) % width, 1)
    halo_cond = pltpu.roll(halo, (width // 2 - 2 * k) % width, 1)
    first = lanes == 0
    last = lanes == width - 1
    pairs = [
        (at(head_pad, -1), at(cond_pad, -1)),
        (at(head_pad, 1), at(cond_pad, 1)),
        (
            jnp.where(first, halo_head, pltpu.roll(head, 1, 1)),
            jnp.where(first, halo_cond, pltpu.roll(conduct, 1, 1)),
        ),
        (
            jnp.where(last, halo_head, pltpu.roll(head, width - 1, 1)),
            jnp.where(last, halo_cond, pltpu.roll(conduct, width - 1, 1)),
        ),
    ]
    flow = faces = None
    for other_head, other_cond in pairs:
        both = conduct + other_cond
        term = both * (head - other_head)
        flow = term if flow is None else flow + term
        faces = both if faces is None else faces + both
    return head, conduct, flow, faces


VERTICAL = 0.5 / (0.5 * LATERAL)


def factor_kernel(
    h_ref, cond_ref, stor_ref, row_even_ref, row_odd_ref, own_ref, lane_even_ref, lane_odd_ref,
    res_hbm, inv_hbm, vert_hbm,
    head_pad, cond_pad, res_ref, inv_ref, vert_ref, halo_ref, sems,
):
    layers, rows, width = h_ref.shape
    outs = copies([(res_ref, res_hbm), (inv_ref, inv_hbm), (vert_ref, vert_hbm)], sems, layers)
    fill_pads(h_ref, cond_ref, row_even_ref, row_odd_ref, head_pad, cond_pad)
    halo_ref[...] = lane_halo(own_ref[...], lane_even_ref[...], lane_odd_ref[...])
    size = HALF if rows % HALF == 0 else rows
    lanes = lax.broadcasted_iota(jnp.int32, (size, width), 1)
    for top in range(0, rows, size):
        span = slice(top, top + size)
        halo = halo_ref[span, :]
        vert_above = flux_above = ratio_above = None
        for k in range(layers):
            head, conduct, flow, faces = lateral_terms(
                k, top, size, head_pad, cond_pad, halo, lanes
            )
            diagonal = stor_ref[k, span, :] + faces
            if k < layers - 1:
                vert = VERTICAL * (conduct + cond_ref[k + 1, span, :])
                flux = vert * (head - h_ref[k + 1, span, :] + 1.0)
                diagonal = diagonal + vert
            else:
                vert = None
                flux = conduct * (2.0 * VERTICAL)
            residual = flux + flow
            if k:
                residual = residual - flux_above
                diagonal = diagonal + vert_above
                diagonal = diagonal - vert_above * ratio_above
            inverse = 1.0 / diagonal
            res_ref[k, span, :] = residual
            inv_ref[k, span, :] = inverse
            if vert is not None:
                vert_ref[k, span, :] = vert
                ratio_above = vert * inverse
            else:
                vert_ref[k, span, :] = jnp.zeros_like(inverse)
            vert_above, flux_above = vert, flux
    for chunk in outs:
        for copy in chunk:
            copy.start()
    for chunk in outs:
        for copy in chunk:
            copy.wait()


def slot_places(ids, width):
    shift = width.bit_length() - 1
    row = ids >> shift
    low = ROW_BLOCK.bit_length() - 1
    return row & (ROW_BLOCK - 1), (row >> low) * width + (ids & (width - 1))


def one_hot(ids, count):
    place = lax.broadcasted_iota(jnp.int32, (count, ids.shape[1]), 0)
    return (place == ids).astype(F32).astype(BF16)


def middle_kernel(
    slots_ref, h_hbm, res_hbm, inv_hbm, vert_hbm,
    alpha_hbm, n1_hbm, half_m_hbm, ksat_hbm, room_hbm, sat_hbm,
    head_ref, cond_ref, stor_ref, source_ref, sink_ref, row_even_ref, row_odd_ref, lane_ref,
    total, left_a, left_b, hot_a, hot_b,
    h_ref, res_ref, inv_ref, vert_ref,
    alpha_ref, n1_ref, half_m_ref, ksat_ref, room_ref, sat_ref, sems,
):
    layers, rows, width = h_ref.shape
    peers, fields, per_peer = slots_ref.shape
    roots = fields - 2
    values = fields - 1
    blocks = rows // ROW_BLOCK
    half = values * ROW_BLOCK
    group = left_a.shape[1] // per_peer
    steps = peers // group
    loads = [
        pltpu.make_async_copy(a, b, sems.at[i])
        for i, (a, b) in enumerate(
            [
                (res_hbm, res_ref), (inv_hbm, inv_ref), (vert_hbm, vert_ref), (h_hbm, h_ref),
                (alpha_hbm, alpha_ref), (n1_hbm, n1_ref), (half_m_hbm, half_m_ref),
                (ksat_hbm, ksat_ref), (room_hbm, room_ref), (sat_hbm, sat_ref),
            ]
        )
    ]
    for copy in loads:
        copy.start()
    total[...] = jnp.zeros_like(total)

    def build(step, left, hot):
        for g in range(group):
            block = slots_ref[step * group + g]
            at = slice(g * per_peer, (g + 1) * per_peer)
            row, column = slot_places(block[values : values + 1, :].astype(jnp.int32), width)
            hot[:, at] = one_hot(column, blocks * width)
            mask = lax.broadcasted_iota(jnp.int32, (ROW_BLOCK, per_peer), 0) == row
            high = block.astype(BF16).astype(F32)
            low = block - high
            for f in range(values):
                for base, part in ((0, high), (half, low)):
                    first = base + f * ROW_BLOCK
                    left[first : first + ROW_BLOCK, at] = jnp.where(
                        mask, part[f : f + 1, :], 0.0
                    ).astype(BF16)

    def add(left, hot):
        total[...] += lax.dot_general(
            left[...], hot[...], (((1,), (1,)), ((), ())), preferred_element_type=F32
        )

    build(0, left_a, hot_a)

    def place(pair, carry):
        build(2 * pair + 1, left_b, hot_b)
        add(left_a, hot_a)
        build(jnp.minimum(2 * pair + 2, steps - 1), left_a, hot_a)
        add(left_b, hot_b)
        return carry

    lax.fori_loop(0, steps // 2, place, 0)
    for copy in loads:
        copy.wait()

    def grid(f, b):
        at = f * ROW_BLOCK
        cols = slice(b * width, (b + 1) * width)
        return total[at : at + ROW_BLOCK, cols] + total[half + at : half + at + ROW_BLOCK, cols]

    even = lax.rem(lax.axis_index("bx"), 2) == 0
    lanes = lax.broadcasted_iota(jnp.int32, (ROW_BLOCK, width), 1)
    for b in range(blocks):
        span = slice(b * ROW_BLOCK, (b + 1) * ROW_BLOCK)
        value = None
        for k in range(layers):
            residual = res_ref[k, span, :]
            if k < roots:
                sink = grid(k, b)
                sink_ref[k, span, :] = sink
                if k == 0:
                    sink = sink - grid(roots, b)
                source_ref[k, span, :] = sink
                residual = residual + sink
            target = -residual
            if k:
                target = target + vert_ref[k - 1, span, :] * value
            value = target * inv_ref[k, span, :]
            head_ref[k, span, :] = value
        change = value
        head_ref[layers - 1, span, :] = h_ref[layers - 1, span, :] + change
        for k in range(layers - 2, -1, -1):
            ratio = vert_ref[k, span, :] * inv_ref[k, span, :]
            change = head_ref[k, span, :] + ratio * change
            head_ref[k, span, :] = h_ref[k, span, :] + change
    for b in range(blocks):
        span = slice(b * ROW_BLOCK, (b + 1) * ROW_BLOCK)
        packed = jnp.zeros((ROW_BLOCK, width), F32)
        for k in range(layers):
            head = head_ref[k, span, :]
            room = room_ref[k, span, :]
            saturation, conduct, storage = closure(
                head, alpha_ref[k, span, :], n1_ref[k, span, :], half_m_ref[k, span, :],
                ksat_ref[k, span, :], room,
            )
            cond_ref[k, span, :] = conduct
            stor_ref[k, span, :] = storage
            source = room * (saturation - sat_ref[k, span, :])
            if k < roots:
                source = source + source_ref[k, span, :]
            source_ref[k, span, :] = source
            packed = edge_messages((head, conduct), k, lanes, packed)
        lane_ref[span, :] = packed
    store_rows(head_ref, cond_ref, even, row_even_ref, row_odd_ref)


def last_kernel(
    slots_ref, old_head_ref, cond_ref, stor_ref, source_ref, sink_ref,
    alpha_hbm, n1_hbm, half_m_hbm,
    row_even_ref, row_odd_ref, own_ref, lane_even_ref, lane_odd_ref,
    head_hbm, reply_ref,
    head_pad, cond_pad, head_ref, ratio_ref, value_ref, alpha_ref, n1_ref, half_m_ref,
    halo_ref, stress_ref, sems,
):
    layers, rows, width = head_ref.shape
    peers, fields, per_peer = slots_ref.shape
    roots = fields - 2
    blocks = rows // ROW_BLOCK
    loads = [
        pltpu.make_async_copy(a, b, sems.at[i])
        for i, (a, b) in enumerate(
            [(alpha_hbm, alpha_ref), (n1_hbm, n1_ref), (half_m_hbm, half_m_ref)]
        )
    ]
    for copy in loads:
        copy.start()
    fill_pads(old_head_ref, cond_ref, row_even_ref, row_odd_ref, head_pad, cond_pad)
    halo_ref[...] = lane_halo(own_ref[...], lane_even_ref[...], lane_odd_ref[...])
    size = HALF if rows % HALF == 0 else rows
    lanes = lax.broadcasted_iota(jnp.int32, (size, width), 1)
    for top in range(0, rows, size):
        span = slice(top, top + size)
        halo = halo_ref[span, :]
        vert_above = flux_above = ratio_above = value = None
        for k in range(layers):
            head, conduct, flow, faces = lateral_terms(
                k, top, size, head_pad, cond_pad, halo, lanes
            )
            diagonal = stor_ref[k, span, :] + faces
            if k < layers - 1:
                vert = VERTICAL * (conduct + cond_ref[k + 1, span, :])
                flux = vert * (head - old_head_ref[k + 1, span, :] + 1.0)
                diagonal = diagonal + vert
            else:
                vert = None
                flux = conduct * (2.0 * VERTICAL)
            residual = flux + flow + source_ref[k, span, :]
            if k:
                residual = residual - flux_above
                diagonal = diagonal + vert_above
                diagonal = diagonal - vert_above * ratio_above
                value = (vert_above * value - residual) * (inverse := 1.0 / diagonal)
            else:
                value = -residual * (inverse := 1.0 / diagonal)
            value_ref[k, span, :] = value
            if vert is not None:
                ratio_above = vert * inverse
                ratio_ref[k, span, :] = ratio_above
            vert_above, flux_above = vert, flux
        if top == 0:
            for copy in loads:
                copy.wait()
        change = value
        head_ref[layers - 1, span, :] = old_head_ref[layers - 1, span, :] + change
        numer = denom = None
        for k in range(layers - 2, -1, -1):
            change = value_ref[k, span, :] + ratio_ref[k, span, :] * change
            head = old_head_ref[k, span, :] + change
            head_ref[k, span, :] = head
            if k < roots:
                half = powers(
                    head, alpha_ref[k, span, :], n1_ref[k, span, :], half_m_ref[k, span, :]
                )[2]
                sink = sink_ref[k, span, :]
                term = sink * jnp.exp2(half + half)
                numer = term if numer is None else numer + term
                denom = sink if denom is None else denom + sink
        held = denom > 0.0
        stress_ref[span, :] = jnp.where(held, numer / jnp.where(held, denom, 1.0), 0.0)
    leave = pltpu.make_async_copy(head_ref, head_hbm, sems.at[3])
    leave.start()
    wide = jnp.concatenate(
        [stress_ref[b * ROW_BLOCK : (b + 1) * ROW_BLOCK, :] for b in range(blocks)], 1
    )
    high = wide.astype(BF16)
    both = jnp.concatenate([high, (wide - high.astype(F32)).astype(BF16)], 0)

    def answer(block, carry):
        for g in range(UNROLL):
            peer = block * UNROLL + g
            ids = slots_ref[peer, fields - 1 : fields, :].astype(jnp.int32)
            row, column = slot_places(ids, width)
            hot = one_hot(column, blocks * width)
            found = jnp.dot(both, hot, preferred_element_type=F32)
            found = found[:ROW_BLOCK] + found[ROW_BLOCK:]
            mask = lax.broadcasted_iota(jnp.int32, (ROW_BLOCK, per_peer), 0) == row
            reply_ref[pl.ds(peer, 1), :] = jnp.sum(
                jnp.where(mask, found, 0.0), 0, keepdims=True
            )
        return carry

    lax.fori_loop(0, peers // UNROLL, answer, 0)
    leave.wait()


def swaps(size):
    even = [(i, i ^ 1) for i in range(size)]
    odd = [(i, (i + 1) % size if i % 2 else (i - 1) % size) for i in range(size)]
    return even, odd


def exchange(row_even, row_odd, packed):
    even_x, odd_x = swaps(lax.axis_size("bx"))
    even_y, odd_y = swaps(lax.axis_size("by"))
    return (
        lax.ppermute(row_even, "bx", even_x),
        lax.ppermute(row_odd, "bx", odd_x),
        packed,
        lax.ppermute(packed, "by", even_y),
        lax.ppermute(packed, "by", odd_y),
    )


VMEM = pltpu.VMEM
HBM = pltpu.HBM


def call(kernel, ins, outs, scratch, name):
    return pl.pallas_call(
        kernel,
        in_specs=[pl.BlockSpec(memory_space=m) for m in ins],
        out_specs=[pl.BlockSpec(memory_space=m) for _, m in outs],
        out_shape=[
            HBM(s, F32) if m is HBM else jax.ShapeDtypeStruct(s, F32) for s, m in outs
        ],
        scratch_shapes=scratch,
        name=name,
        compiler_params=pltpu.CompilerParams(vmem_limit_bytes=20 * MIB),
    )


def in_hbm(*arrays):
    return [pltpu.with_memory_space_constraint(a, HBM) for a in arrays]


def prepare(root_fraction, transpiration, infiltration, clump_cell, peers, per_peer):
    roots, slot_count = root_fraction.shape
    steps = 4 if peers % 4 == 0 else 1
    span = slot_count // steps
    line = pl.BlockSpec((1, span), lambda i: (0, i))
    return pl.pallas_call(
        prepare_kernel,
        grid=(steps,),
        in_specs=[pl.BlockSpec((roots, span), lambda i: (0, i)), line, line, line],
        out_specs=pl.BlockSpec((peers // steps, roots + 2, per_peer), lambda i: (i, 0, 0)),
        out_shape=jax.ShapeDtypeStruct((peers, roots + 2, per_peer), F32),
        name="prepare",
        compiler_params=pltpu.CompilerParams(vmem_limit_bytes=4 * MIB),
    )(*in_hbm(root_fraction, transpiration[None], infiltration[None], clump_cell[None]))


def on_device(
    h_old,
    soil_type,
    ks_scale,
    soil_table,
    clump_brick,
    clump_cell,
    root_fraction,
    transpiration,
    infiltration,
):
    layers, rows, width = h_old.shape
    peers = lax.axis_size("bx") * lax.axis_size("by")
    roots, slot_count = root_fraction.shape
    per_peer = slot_count // peers
    cells = (layers, rows, width)
    row_msg = (2, layers, width)
    lane_msg = (rows, width)
    axes = ("bx", "by")
    on_chip = lambda *shapes: [(s, VMEM) for s in shapes]
    buffers = lambda n: [VMEM(cells, F32)] * n
    semaphores = pltpu.SemaphoreType.DMA
    chunks = len(layer_chunks(layers))

    slots = lax.all_to_all(
        prepare(root_fraction, transpiration, infiltration, clump_cell, peers, per_peer),
        axes,
        split_axis=0,
        concat_axis=0,
        tiled=True,
    )
    table = jnp.pad(soil_table, ((0, 0), (0, width - soil_table.shape[1])))
    alpha, n1, half_m, ksat, room, sat, head, conduct, storage, row_even, row_odd, packed = call(
        first_kernel,
        [HBM] * 3 + [VMEM],
        [(cells, HBM)] * 6 + on_chip(cells, cells, cells, row_msg, row_msg, lane_msg),
        [VMEM(cells, jnp.int32)] + buffers(7) + [semaphores((3 * chunks,)), semaphores((6 * chunks,))],
        "first",
    )(*in_hbm(h_old, soil_type, ks_scale), table)
    pads = [VMEM((layers, rows + 2 * PAD, width), F32)] * 2
    residual, inverse, vert = call(
        factor_kernel,
        [VMEM] * 8,
        [(cells, HBM)] * 3,
        pads + buffers(3) + [VMEM(lane_msg, F32), semaphores((3 * chunks,))],
        "factor",
    )(head, conduct, storage, *exchange(row_even, row_odd, packed))
    values = roots + 1
    columns = rows // ROW_BLOCK * width
    group = GROUP if peers % (2 * GROUP) == 0 else 1
    lefts = [VMEM((2 * values * ROW_BLOCK, group * per_peer), BF16)] * 2
    hots = [VMEM((columns, group * per_peer), BF16)] * 2
    head, conduct, storage, source, sink, row_even, row_odd, packed = call(
        middle_kernel,
        [VMEM] + [HBM] * 10,
        on_chip(*[cells] * 4, (roots, rows, width), row_msg, row_msg, lane_msg),
        [VMEM((2 * values * ROW_BLOCK, columns), F32)] + lefts + hots
        + buffers(10) + [semaphores((10,))],
        "middle",
    )(slots, *in_hbm(h_old, residual, inverse, vert, alpha, n1, half_m, ksat, room, sat))
    head, reply = call(
        last_kernel,
        [VMEM] * 6 + [HBM] * 3 + [VMEM] * 5,
        [(cells, HBM), ((peers, per_peer), VMEM)],
        pads + buffers(6) + [VMEM(lane_msg, F32)] * 2 + [semaphores((4,))],
        "last",
    )(
        slots, head, conduct, storage, source, sink, *in_hbm(alpha, n1, half_m),
        *exchange(row_even, row_odd, packed),
    )
    stress = lax.all_to_all(reply, axes, split_axis=0, concat_axis=0, tiled=True)
    return head, stress.reshape(slot_count)


def solution(mesh):
    placed = (
        P(None, "bx", "by"),
        P(None, "bx", "by"),
        P(None, "bx", "by"),
        P(),
        P(("bx", "by")),
        P(("bx", "by")),
        P(None, ("bx", "by")),
        P(("bx", "by")),
        P(("bx", "by")),
    )
    return jax.shard_map(
        on_device,
        mesh=mesh,
        in_specs=placed,
        out_specs=(P(None, "bx", "by"), P(("bx", "by"))),
        check_vma=False,
    )
```

```python
import jax
import jax.numpy as jnp
from jax import lax
from jax.experimental import pallas as pl
from jax.experimental.pallas import tpu as pltpu
from jax.sharding import PartitionSpec as P

ITERS = 2
RESIDUAL_WATER = 0.05
STORAGE = 0.2
TIME_STEP = 0.5
LATERAL = 0.5
TINY = 1e-30
ROW_BLOCK = 32
HALF = 32
UNROLL = 8
GROUP = 4
LOG2E = 1.4426950408889634
PAD = 8
F32 = jnp.float32
BF16 = jnp.bfloat16
MIB = 1 << 20
VMEM = pltpu.VMEM
HBM = pltpu.HBM


def lane_tables(table, shape):
    t0, t1, t2, t3 = (table[i : i + 1, :] for i in range(4))
    alpha = 4.0 * t0
    n1 = 0.2 + 2.0 * t1
    half_m = 0.5 * n1 / (1.0 + n1)
    ks3 = (0.5 * LATERAL * 3.0) * t2
    room = ((0.3 - RESIDUAL_WATER) + 0.3 * t3) * (1.0 / TIME_STEP)
    rows = (alpha, LOG2E * n1, -LOG2E * half_m, ks3, room)
    return [jnp.broadcast_to(r, shape) for r in rows]


def powers(head, alpha, n1, half_m):
    suction = jnp.maximum(alpha * jnp.maximum(-head, 0.0), TINY)
    power = jnp.exp2(n1 * lax.log(suction))
    log_base = lax.log(1.0 + suction * power)
    return power, log_base, half_m * log_base


def closure(head, alpha, n1, half_m, ksat, room):
    power, log_base, half = powers(head, alpha, n1, half_m)
    root = jnp.exp2(half)
    saturation = root * root
    share = power * saturation
    inner = 1.0 - share
    conduct = (ksat * root) * (inner * inner)
    cap = (room * (1.0 / LOG2E)) * (n1 * alpha)
    storage = STORAGE / TIME_STEP + cap * (share * jnp.exp2(-LOG2E * log_base))
    return saturation, conduct, storage


def lane_lookup(row, index):
    return jnp.take_along_axis(row, index, axis=1, mode="promise_in_bounds")


def conductivity(head, alpha, n1, half_m, ksat):
    power, _, half = powers(head, alpha, n1, half_m)
    root = jnp.exp2(half)
    inner = 1.0 - power * (root * root)
    return (ksat * root) * (inner * inner)


def edge_lanes(values, k, layers, lanes, packed):
    for part, value in enumerate(values):
        at = 2 * (part * layers + k)
        moved = pltpu.roll(value, at + 1, 1)
        packed = jnp.where((lanes == at) | (lanes == at + 1), moved, packed)
    return packed


def edge_rows(refs, row_even_ref, row_odd_ref):
    even = lax.rem(lax.axis_index("bx"), 2) == 0
    for part, ref in enumerate(refs):
        rows = ref.shape[1]
        low = ref[:, 0, :].astype(F32)
        high = ref[:, rows - 1, :].astype(F32)
        row_even_ref[part] = jnp.where(even, high, low)
        row_odd_ref[part] = jnp.where(even, low, high)


def row_halo(own_even, own_odd, row_even, row_odd):
    index = lax.axis_index("bx")
    even = lax.rem(index, 2) == 0
    low = jnp.where(even, row_odd, row_even)
    high = jnp.where(even, row_even, row_odd)
    own_low = jnp.where(even, own_odd, own_even)
    own_high = jnp.where(even, own_even, own_odd)
    low = jnp.where(index == 0, own_low, low)
    high = jnp.where(index == lax.axis_size("bx") - 1, own_high, high)
    return low, high


def lane_halo(own, lane_even, lane_odd):
    index = lax.axis_index("by")
    even = lax.rem(index, 2) == 0
    width = own.shape[1]
    lanes = lax.broadcasted_iota(jnp.int32, own.shape, 1)
    low = jnp.where(even, lane_odd, lane_even)
    high = jnp.where(even, lane_even, lane_odd)
    low = jnp.where(index == 0, pltpu.roll(own, width - 1, 1), low)
    high = jnp.where(index == lax.axis_size("by") - 1, pltpu.roll(own, 1, 1), high)
    return jnp.where(lax.rem(lanes, 2) == 0, low, pltpu.roll(high, width - 2, 1))


def edge_signs(shape):
    x, y = lax.axis_index("bx"), lax.axis_index("by")
    minus = lambda at_edge: jnp.where(at_edge, -1.0, 1.0)
    lanes = lax.broadcasted_iota(jnp.int32, shape, 1)
    return (
        minus(x == 0),
        minus(x == lax.axis_size("bx") - 1),
        jnp.where(
            lax.rem(lanes, 2) == 0, minus(y == 0), minus(y == lax.axis_size("by") - 1)
        ),
    )


def prepare_kernel(
    root_hbm, transp_hbm, infil_hbm, cell_hbm, out_ref,
    root_ref, transp_ref, infil_ref, cell_ref, sems,
):
    peers, fields, per_peer = out_ref.shape
    roots = fields - 2
    steps = 4 if peers % 4 == 0 else 1
    span = peers // steps * per_peer
    lines = [
        pltpu.make_async_copy(a, b, sems.at[steps + i])
        for i, (a, b) in enumerate(
            [(transp_hbm, transp_ref), (infil_hbm, infil_ref), (cell_hbm, cell_ref)]
        )
    ]
    parts = [
        pltpu.make_async_copy(
            root_hbm.at[:, pl.ds(i * span, span)],
            root_ref.at[:, pl.ds(i * span, span)],
            sems.at[i],
        )
        for i in range(steps)
    ]
    for copy in lines + parts:
        copy.start()
    for copy in lines:
        copy.wait()
    for i, copy in enumerate(parts):
        copy.wait()
        for peer in range(i * peers // steps, (i + 1) * peers // steps):
            at = slice(peer * per_peer, (peer + 1) * per_peer)
            out_ref[peer, :roots, :] = root_ref[:, at] * transp_ref[:, at]
            out_ref[peer, roots : roots + 1, :] = infil_ref[:, at]
            out_ref[peer, roots + 1 :, :] = cell_ref[:, at].astype(F32)


def layer_chunks(layers):
    size = 5 if layers % 5 == 0 else layers
    return [(at, size) for at in range(0, layers, size)]


def copies(pairs, sems, layers):
    chunks = layer_chunks(layers)
    return [
        [
            pltpu.make_async_copy(
                a.at[pl.ds(at, size)], b.at[pl.ds(at, size)], sems.at[c * len(pairs) + i]
            )
            for i, (a, b) in enumerate(pairs)
        ]
        for c, (at, size) in enumerate(chunks)
    ]


def edges_kernel(
    h_hbm, soil_hbm, ks_hbm,
    h_ref, soil_ref, ks_ref, row_even_ref, row_odd_ref, lane_ref,
    sems,
):
    layers, rows, width = h_ref.shape
    ins = copies([(h_hbm, h_ref), (soil_hbm, soil_ref), (ks_hbm, ks_ref)], sems, layers)
    for chunk in ins:
        for copy in chunk:
            copy.start()
    lanes = lax.broadcasted_iota(jnp.int32, (rows, width), 1)
    packed = jnp.zeros((rows, width), F32)
    for (at, size), arrive in zip(layer_chunks(layers), ins):
        for copy in arrive:
            copy.wait()
        for k in range(at, at + size):
            packed = edge_lanes(
                (h_ref[k], soil_ref[k].astype(F32), ks_ref[k]), k, layers, lanes, packed
            )
    lane_ref[...] = packed
    edge_rows((h_ref, soil_ref, ks_ref), row_even_ref, row_odd_ref)


def lateral_terms(k, top, size, head_pad, cond_pad, halo_head, halo_cond, lanes):
    width = head_pad.shape[2]
    at = lambda pad, move: pad[k, PAD + top + move : PAD + top + move + size, :]
    head, conduct = at(head_pad, 0), at(cond_pad, 0)
    halo_head = pltpu.roll(halo_head, (width - 2 * k) % width, 1)
    halo_cond = pltpu.roll(halo_cond, (width - 2 * k) % width, 1)
    first = lanes == 0
    last = lanes == width - 1
    pairs = [
        (at(head_pad, -1), at(cond_pad, -1)),
        (at(head_pad, 1), at(cond_pad, 1)),
        (
            jnp.where(first, halo_head, pltpu.roll(head, 1, 1)),
            jnp.where(first, halo_cond, pltpu.roll(conduct, 1, 1)),
        ),
        (
            jnp.where(last, halo_head, pltpu.roll(head, width - 1, 1)),
            jnp.where(last, halo_cond, pltpu.roll(conduct, width - 1, 1)),
        ),
    ]
    flow = faces = None
    for other_head, other_cond in pairs:
        both = conduct + other_cond
        term = both * (head - other_head)
        flow = term if flow is None else flow + term
        faces = both if faces is None else faces + both
    return head, conduct, flow, faces


VERTICAL = 0.5 / (0.5 * LATERAL)


def first_kernel(
    h_ref, soil_ref, ks_ref, table_ref,
    alpha_hbm, n1_hbm, half_m_hbm, ksat_hbm, room_hbm, sat_ref, cond_ref, stor_ref,
    alpha_ref, n1_ref, half_m_ref, ksat_ref, room_ref, sems,
):
    layers, rows, width = h_ref.shape
    outs = copies(
        [
            (alpha_ref, alpha_hbm), (n1_ref, n1_hbm), (half_m_ref, half_m_hbm),
            (ksat_ref, ksat_hbm), (room_ref, room_hbm),
        ],
        sems,
        layers,
    )
    tables = lane_tables(table_ref[...], (8, width))
    for (at, size), leave in zip(layer_chunks(layers), outs):
        for k in range(at, at + size):
            for row in range(0, rows, 8):
                span = slice(row, row + 8)
                kind = soil_ref[k, span, :]
                alpha, n1, half_m, ks3, room = (lane_lookup(t, kind) for t in tables)
                ksat = ks3 * ks_ref[k, span, :]
                alpha_ref[k, span, :] = alpha
                n1_ref[k, span, :] = n1
                half_m_ref[k, span, :] = half_m
                ksat_ref[k, span, :] = ksat
                room_ref[k, span, :] = room
                saturation, conduct, storage = closure(
                    h_ref[k, span, :], alpha, n1, half_m, ksat, room
                )
                sat_ref[k, span, :] = saturation
                cond_ref[k, span, :] = conduct
                stor_ref[k, span, :] = storage
        for copy in leave:
            copy.start()
    for chunk in outs:
        for copy in chunk:
            copy.wait()


def factor_kernel(
    h_ref, cond_ref, stor_ref, table_ref,
    own_even_ref, own_odd_ref, row_even_ref, row_odd_ref, own_ref, lane_even_ref, lane_odd_ref,
    res_ref, inv_ref, vert_ref, row_par_ref, lane_par_ref,
    head_pad, cond_pad, halo_ref,
):
    layers, rows, width = h_ref.shape
    head_pad[:, PAD : PAD + rows, :] = h_ref[...]
    cond_pad[:, PAD : PAD + rows, :] = cond_ref[...]
    sign_low, sign_high, sign_lane = edge_signs((rows, width))
    kinds = lambda x: jnp.clip(x.astype(jnp.int32), 0, width - 1)
    for side, sign in ((0, sign_low), (1, sign_high)):
        head, kind, ks = (
            row_halo(own_even_ref[i], own_odd_ref[i], row_even_ref[i], row_odd_ref[i])[side]
            for i in range(3)
        )
        wide = lane_tables(table_ref[...], head.shape)[:4]
        pars = [lane_lookup(t, kinds(kind)) for t in wide]
        pars[3] = sign * (pars[3] * ks)
        for i in range(4):
            row_par_ref[side, i] = pars[i]
        row = PAD - 1 if side == 0 else PAD + rows
        head_pad[:, row, :] = head
        cond_pad[:, row, :] = conductivity(head, *pars)
    halo = lane_halo(own_ref[...], lane_even_ref[...], lane_odd_ref[...])
    wide = lane_tables(table_ref[...], halo.shape)[:4]
    kind = kinds(pltpu.roll(halo, width - 2 * layers, 1))
    pars = [lane_lookup(t, kind) for t in wide]
    pars[3] = sign_lane * (pars[3] * pltpu.roll(halo, width - 4 * layers, 1))
    for i in range(4):
        lane_par_ref[i] = pars[i]
    halo_ref[0] = halo
    halo_ref[1] = conductivity(halo, *pars)
    size = HALF if rows % HALF == 0 else rows
    lanes = lax.broadcasted_iota(jnp.int32, (size, width), 1)
    for top in range(0, rows, size):
        span = slice(top, top + size)
        inner = slice(PAD + top, PAD + top + size)
        vert_above = flux_above = ratio_above = None
        for k in range(layers):
            head, conduct, flow, faces = lateral_terms(
                k, top, size, head_pad, cond_pad, halo_ref[0, span], halo_ref[1, span], lanes
            )
            diagonal = stor_ref[k, span, :] + faces
            if k < layers - 1:
                vert = VERTICAL * (conduct + cond_pad[k + 1, inner, :])
                flux = vert * (head - head_pad[k + 1, inner, :] + 1.0)
                diagonal = diagonal + vert
            else:
                vert = None
                flux = conduct * (2.0 * VERTICAL)
            residual = flux + flow
            if k:
                residual = residual - flux_above
                diagonal = diagonal + vert_above
                diagonal = diagonal - vert_above * ratio_above
            inverse = 1.0 / diagonal
            res_ref[k, span, :] = residual
            inv_ref[k, span, :] = inverse
            if vert is not None:
                vert_ref[k, span, :] = vert
                ratio_above = vert * inverse
            vert_above, flux_above = vert, flux


def slot_places(ids, width):
    shift = width.bit_length() - 1
    row = ids >> shift
    low = ROW_BLOCK.bit_length() - 1
    return row & (ROW_BLOCK - 1), (row >> low) * width + (ids & (width - 1))


def one_hot(ids, count):
    place = lax.broadcasted_iota(jnp.int32, (count, ids.shape[1]), 0)
    return (place == ids).astype(F32).astype(BF16)


def middle_kernel(
    slots_ref, h_hbm, alpha_hbm, n1_hbm, half_m_hbm, ksat_hbm, room_hbm,
    res_ref, inv_ref, vert_ref,
    head_ref, sink_ref, infil_ref, row_even_ref, row_odd_ref, lane_ref,
    alpha_ref, n1_ref, half_m_ref, ksat_ref, room_ref,
    total, left_a, left_b, hot_a, hot_b, h_ref, sems,
):
    layers, rows, width = h_ref.shape
    peers, fields, per_peer = slots_ref.shape
    roots = fields - 2
    values = fields - 1
    blocks = rows // ROW_BLOCK
    half = values * ROW_BLOCK
    group = left_a.shape[1] // per_peer
    steps = peers // group
    loads = [
        pltpu.make_async_copy(a, b, sems.at[i])
        for i, (a, b) in enumerate(
            [
                (h_hbm, h_ref),
                (alpha_hbm, alpha_ref), (n1_hbm, n1_ref), (half_m_hbm, half_m_ref),
                (ksat_hbm, ksat_ref), (room_hbm, room_ref),
            ]
        )
    ]
    for copy in loads:
        copy.start()
    total[...] = jnp.zeros_like(total)

    def build(step, left, hot):
        for g in range(group):
            block = slots_ref[step * group + g]
            at = slice(g * per_peer, (g + 1) * per_peer)
            row, column = slot_places(block[values : values + 1, :].astype(jnp.int32), width)
            hot[:, at] = one_hot(column, blocks * width)
            mask = lax.broadcasted_iota(jnp.int32, (ROW_BLOCK, per_peer), 0) == row
            high = block.astype(BF16).astype(F32)
            low = block - high
            for f in range(values):
                for base, part in ((0, high), (half, low)):
                    first = base + f * ROW_BLOCK
                    left[first : first + ROW_BLOCK, at] = jnp.where(
                        mask, part[f : f + 1, :], 0.0
                    ).astype(BF16)

    def add(left, hot):
        total[...] += lax.dot_general(
            left[...], hot[...], (((1,), (1,)), ((), ())), preferred_element_type=F32
        )

    build(0, left_a, hot_a)

    def place(pair, carry):
        build(2 * pair + 1, left_b, hot_b)
        add(left_a, hot_a)
        build(jnp.minimum(2 * pair + 2, steps - 1), left_a, hot_a)
        add(left_b, hot_b)
        return carry

    lax.fori_loop(0, steps // 2, place, 0)
    for copy in loads:
        copy.wait()

    def grid(f, b):
        at = f * ROW_BLOCK
        cols = slice(b * width, (b + 1) * width)
        return total[at : at + ROW_BLOCK, cols] + total[half + at : half + at + ROW_BLOCK, cols]

    lanes = lax.broadcasted_iota(jnp.int32, (ROW_BLOCK, width), 1)
    for b in range(blocks):
        span = slice(b * ROW_BLOCK, (b + 1) * ROW_BLOCK)
        packed = jnp.zeros((ROW_BLOCK, width), F32)
        infil = grid(roots, b)
        infil_ref[span, :] = infil
        value = None
        for k in range(layers):
            target = -res_ref[k, span, :]
            if k < roots:
                sink = grid(k, b)
                sink_ref[k, span, :] = sink
                target = target - sink
            if k == 0:
                target = target + infil
            else:
                target = target + vert_ref[k - 1, span, :] * value
            value = target * inv_ref[k, span, :]
            head_ref[k, span, :] = value
        change = value
        for k in range(layers - 1, -1, -1):
            if k < layers - 1:
                ratio = vert_ref[k, span, :] * inv_ref[k, span, :]
                change = head_ref[k, span, :] + ratio * change
            head = h_ref[k, span, :] + change
            head_ref[k, span, :] = head
            packed = edge_lanes((head,), k, layers, lanes, packed)
        lane_ref[span, :] = packed
    edge_rows((head_ref,), row_even_ref, row_odd_ref)


def close_kernel(
    head_ref, sink_ref, infil_ref,
    alpha_ref, n1_ref, half_m_ref, ksat_ref, room_ref, sat_ref,
    cond_ref, stor_ref, source_ref,
):
    layers, rows, width = head_ref.shape
    roots = sink_ref.shape[0]
    for k in range(layers):
        room = room_ref[k]
        saturation, conduct, storage = closure(
            head_ref[k], alpha_ref[k], n1_ref[k], half_m_ref[k], ksat_ref[k], room
        )
        cond_ref[k] = conduct
        stor_ref[k] = storage
        source = room * (saturation - sat_ref[k])
        if k < roots:
            source = source + sink_ref[k]
        if k == 0:
            source = source - infil_ref[...]
        source_ref[k] = source


def last_kernel(
    slots_ref, old_head_ref, cond_ref, stor_ref, source_ref, sink_ref,
    alpha_ref, n1_ref, half_m_ref, row_par_ref, lane_par_ref,
    own_even_ref, own_odd_ref, row_even_ref, row_odd_ref, own_ref, lane_even_ref, lane_odd_ref,
    head_hbm, reply_ref,
    head_pad, cond_pad, head_ref, ratio_ref, value_ref, halo_ref, stress_ref, sems,
):
    layers, rows, width = head_ref.shape
    peers, fields, per_peer = slots_ref.shape
    roots = fields - 2
    blocks = rows // ROW_BLOCK
    head_pad[:, PAD : PAD + rows, :] = old_head_ref[...]
    cond_pad[:, PAD : PAD + rows, :] = cond_ref[...]
    sides = row_halo(own_even_ref[0], own_odd_ref[0], row_even_ref[0], row_odd_ref[0])
    for side, row in ((0, PAD - 1), (1, PAD + rows)):
        head_pad[:, row, :] = sides[side]
        pars = [row_par_ref[side, i] for i in range(4)]
        cond_pad[:, row, :] = conductivity(sides[side], *pars)
    halo = lane_halo(own_ref[...], lane_even_ref[...], lane_odd_ref[...])
    halo_ref[0] = halo
    halo_ref[1] = conductivity(halo, *(lane_par_ref[i] for i in range(4)))
    size = HALF if rows % HALF == 0 else rows
    lanes = lax.broadcasted_iota(jnp.int32, (size, width), 1)
    for top in range(0, rows, size):
        span = slice(top, top + size)
        vert_above = flux_above = ratio_above = value = None
        for k in range(layers):
            head, conduct, flow, faces = lateral_terms(
                k, top, size, head_pad, cond_pad, halo_ref[0, span], halo_ref[1, span], lanes
            )
            diagonal = stor_ref[k, span, :] + faces
            if k < layers - 1:
                vert = VERTICAL * (conduct + cond_ref[k + 1, span, :])
                flux = vert * (head - old_head_ref[k + 1, span, :] + 1.0)
                diagonal = diagonal + vert
            else:
                vert = None
                flux = conduct * (2.0 * VERTICAL)
            residual = flux + flow + source_ref[k, span, :]
            if k:
                residual = residual - flux_above
                diagonal = diagonal + vert_above
                diagonal = diagonal - vert_above * ratio_above
                inverse = 1.0 / diagonal
                value = (vert_above * value - residual) * inverse
            else:
                inverse = 1.0 / diagonal
                value = -residual * inverse
            value_ref[k, span, :] = value
            if vert is not None:
                ratio_above = vert * inverse
                ratio_ref[k, span, :] = ratio_above
            vert_above, flux_above = vert, flux
        change = value
        head_ref[layers - 1, span, :] = old_head_ref[layers - 1, span, :] + change
        numer = denom = None
        for k in range(layers - 2, -1, -1):
            change = value_ref[k, span, :] + ratio_ref[k, span, :] * change
            head = old_head_ref[k, span, :] + change
            head_ref[k, span, :] = head
            if k < roots:
                half = powers(
                    head, alpha_ref[k, span, :], n1_ref[k, span, :], half_m_ref[k, span, :]
                )[2]
                sink = sink_ref[k, span, :]
                term = sink * jnp.exp2(half + half)
                numer = term if numer is None else numer + term
                denom = sink if denom is None else denom + sink
        held = denom > 0.0
        stress_ref[span, :] = jnp.where(held, numer / jnp.where(held, denom, 1.0), 0.0)
    leave = pltpu.make_async_copy(head_ref, head_hbm, sems.at[0])
    leave.start()
    wide = jnp.concatenate(
        [stress_ref[b * ROW_BLOCK : (b + 1) * ROW_BLOCK, :] for b in range(blocks)], 1
    )
    high = wide.astype(BF16)
    both = jnp.concatenate([high, (wide - high.astype(F32)).astype(BF16)], 0)

    def answer(block, carry):
        for g in range(UNROLL):
            peer = block * UNROLL + g
            ids = slots_ref[peer, fields - 1 : fields, :].astype(jnp.int32)
            row, column = slot_places(ids, width)
            hot = one_hot(column, blocks * width)
            found = jnp.dot(both, hot, preferred_element_type=F32)
            found = found[:ROW_BLOCK] + found[ROW_BLOCK:]
            mask = lax.broadcasted_iota(jnp.int32, (ROW_BLOCK, per_peer), 0) == row
            reply_ref[pl.ds(peer, 1), :] = jnp.sum(
                jnp.where(mask, found, 0.0), 0, keepdims=True
            )
        return carry

    lax.fori_loop(0, peers // UNROLL, answer, 0)
    leave.wait()


def swaps():
    count_x, count_y = lax.axis_size("bx"), lax.axis_size("by")

    def pairs(partner):
        return [
            (x * count_y + y, px * count_y + py)
            for x in range(count_x)
            for y in range(count_y)
            for px, py in [partner(x, y)]
        ]

    odd = lambda i: i + 1 if i % 2 else i - 1
    return (
        pairs(lambda x, y: (x ^ 1, y)),
        pairs(lambda x, y: (odd(x) % count_x, y)),
        pairs(lambda x, y: (x, y ^ 1)),
        pairs(lambda x, y: (x, odd(y)) if 0 < y < count_y - 1 else (x ^ 1, y)),
    )


def exchange(row_even, row_odd, packed):
    even_x, odd_x, even_y, odd_y = swaps()
    axes = ("bx", "by")
    return (
        row_even,
        row_odd,
        lax.ppermute(row_even, axes, even_x),
        lax.ppermute(row_odd, axes, odd_x),
        packed,
        lax.ppermute(packed, axes, even_y),
        lax.ppermute(packed, axes, odd_y),
    )


def call(kernel, ins, outs, scratch, name, limit=20, flops=0):
    return pl.pallas_call(
        kernel,
        in_specs=[pl.BlockSpec(memory_space=m) for m in ins],
        out_specs=[pl.BlockSpec(memory_space=m) for _, _, m in outs],
        out_shape=[HBM(s, t) if m is HBM else jax.ShapeDtypeStruct(s, t) for s, t, m in outs],
        scratch_shapes=scratch,
        name=name,
        cost_estimate=pl.CostEstimate(flops=flops, bytes_accessed=flops, transcendentals=0),
        compiler_params=pltpu.CompilerParams(vmem_limit_bytes=limit * MIB),
    )


def in_hbm(*arrays):
    return [pltpu.with_memory_space_constraint(a, HBM) for a in arrays]


def prepare(root_fraction, transpiration, infiltration, clump_cell, peers, per_peer):
    roots, slot_count = root_fraction.shape
    line = (1, slot_count)
    return pl.pallas_call(
        prepare_kernel,
        in_specs=[pl.BlockSpec(memory_space=HBM)] * 4,
        out_specs=pl.BlockSpec(memory_space=VMEM),
        out_shape=VMEM((peers, roots + 2, per_peer), F32),
        scratch_shapes=[
            VMEM(root_fraction.shape, F32), VMEM(line, F32), VMEM(line, F32),
            VMEM(line, jnp.int32), pltpu.SemaphoreType.DMA((8,)),
        ],
        name="prepare",
        compiler_params=pltpu.CompilerParams(vmem_limit_bytes=6 * MIB),
    )(*in_hbm(root_fraction, transpiration[None], infiltration[None], clump_cell[None]))


def on_device(
    h_old,
    soil_type,
    ks_scale,
    soil_table,
    clump_brick,
    clump_cell,
    root_fraction,
    transpiration,
    infiltration,
):
    layers, rows, width = h_old.shape
    peers = lax.axis_size("bx") * lax.axis_size("by")
    roots, slot_count = root_fraction.shape
    per_peer = slot_count // peers
    cells = (layers, rows, width)
    lane_msg = (rows, width)
    axes = ("bx", "by")
    on_chip = lambda *shapes: [(s, F32, VMEM) for s in shapes]
    in_main = lambda *shapes: [(s, F32, HBM) for s in shapes]
    buffers = lambda n: [VMEM(cells, F32)] * n
    semaphores = pltpu.SemaphoreType.DMA
    chunks = len(layer_chunks(layers))

    slots = lax.all_to_all(
        prepare(root_fraction, transpiration, infiltration, clump_cell, peers, per_peer),
        axes,
        split_axis=0,
        concat_axis=0,
        tiled=True,
    )
    table = jnp.pad(soil_table, ((0, 0), (0, width - soil_table.shape[1])))
    raw_msg = (3, layers, width)
    head, soil, scale, row_even, row_odd, packed = call(
        edges_kernel,
        [HBM] * 3,
        on_chip(cells) + [(cells, jnp.int32, VMEM)] + on_chip(cells, raw_msg, raw_msg, lane_msg),
        [semaphores((3 * chunks,))],
        "edges",
    )(*in_hbm(h_old, soil_type, ks_scale))
    pads = [VMEM((layers, rows + 2 * PAD, width), F32)] * 2
    halo = [VMEM((2,) + lane_msg, F32)]
    arrived = exchange(row_even, row_odd, packed)
    alpha, n1, half_m, ksat, room, old_sat, conduct, storage = call(
        first_kernel,
        [VMEM] * 4,
        in_main(*[cells] * 5) + on_chip(*[cells] * 3),
        buffers(5) + [semaphores((5 * chunks,))],
        "first",
        flops=8_000_000,
    )(head, soil, scale, table)
    residual, inverse, vert, row_par, lane_par = call(
        factor_kernel,
        [VMEM] * 11,
        on_chip(*[cells] * 3, (2, 4, layers, width), (4,) + lane_msg),
        pads + halo,
        "factor",
        flops=4_000_000,
    )(head, conduct, storage, table, *arrived)
    values = roots + 1
    columns = rows // ROW_BLOCK * width
    group = GROUP if peers % (2 * GROUP) == 0 else 1
    lefts = [VMEM((2 * values * ROW_BLOCK, group * per_peer), BF16)] * 2
    hots = [VMEM((columns, group * per_peer), BF16)] * 2
    row_msg = (1, layers, width)
    head, sink, infil, row_even, row_odd, packed, alpha, n1, half_m, ksat, room = call(
        middle_kernel,
        [VMEM] + [HBM] * 6 + [VMEM] * 3,
        on_chip(cells, (roots, rows, width), lane_msg, row_msg, row_msg, lane_msg)
        + on_chip(*[cells] * 5),
        [VMEM((2 * values * ROW_BLOCK, columns), F32)] + lefts + hots
        + buffers(1) + [semaphores((6,))],
        "middle",
    )(
        slots, *in_hbm(h_old, alpha, n1, half_m, ksat, room), residual, inverse, vert
    )
    arrived = exchange(row_even, row_odd, packed)
    conduct, storage, source = call(
        close_kernel, [VMEM] * 9, on_chip(*[cells] * 3), [], "close", limit=4, flops=4_000_000
    )(head, sink, infil, alpha, n1, half_m, ksat, room, old_sat)
    head, reply = call(
        last_kernel,
        [VMEM] * 18,
        in_main(cells) + on_chip((peers, per_peer)),
        pads + buffers(3) + halo + [VMEM(lane_msg, F32), semaphores((1,))],
        "last",
    )(
        slots, head, conduct, storage, source, sink, alpha, n1, half_m, row_par, lane_par,
        *arrived,
    )
    stress = lax.all_to_all(reply, axes, split_axis=0, concat_axis=0, tiled=True)
    return head, stress.reshape(slot_count)


def solution(mesh):
    placed = (
        P(None, "bx", "by"),
        P(None, "bx", "by"),
        P(None, "bx", "by"),
        P(),
        P(("bx", "by")),
        P(("bx", "by")),
        P(None, ("bx", "by")),
        P(("bx", "by")),
        P(("bx", "by")),
    )
    return jax.shard_map(
        on_device,
        mesh=mesh,
        in_specs=placed,
        out_specs=(P(None, "bx", "by"), P(("bx", "by"))),
        check_vma=False,
    )
```

```python
import jax
import jax.numpy as jnp
from jax import lax
from jax.experimental import pallas as pl
from jax.experimental.pallas import tpu as pltpu
from jax.sharding import PartitionSpec as P


RESIDUAL_WATER = 0.05
STORAGE = 0.2
TIME_STEP = 0.5
LATERAL = 0.5
TINY = 1e-30
ROW_BLOCK = 32
HALF = 32
UNROLL = 8
GROUP = 4
LOG2E = 1.4426950408889634
PAD = 8
F32 = jnp.float32
BF16 = jnp.bfloat16
MIB = 1 << 20
VMEM = pltpu.VMEM
HBM = pltpu.HBM


def lane_tables(table, shape):
    t0, t1, t2, t3 = (table[i : i + 1, :] for i in range(4))
    alpha = 4.0 * t0
    n1 = 0.2 + 2.0 * t1
    half_m = 0.5 * n1 / (1.0 + n1)
    ks3 = (0.5 * LATERAL * 3.0) * t2
    room = ((0.3 - RESIDUAL_WATER) + 0.3 * t3) * (1.0 / TIME_STEP)
    rows = (alpha, LOG2E * n1, -LOG2E * half_m, ks3, room)
    return [jnp.broadcast_to(r, shape) for r in rows]


def powers(head, alpha, n1, half_m):
    suction = jnp.maximum(alpha * jnp.maximum(-head, 0.0), TINY)
    power = jnp.exp2(n1 * lax.log(suction))
    log_base = lax.log(1.0 + suction * power)
    return power, log_base, half_m * log_base


def closure(head, alpha, n1, half_m, ksat, room):
    power, log_base, half = powers(head, alpha, n1, half_m)
    root = jnp.exp2(half)
    saturation = root * root
    share = power * saturation
    inner = 1.0 - share
    conduct = (ksat * root) * (inner * inner)
    cap = (room * (1.0 / LOG2E)) * (n1 * alpha)
    storage = STORAGE / TIME_STEP + cap * (share * jnp.exp2(-LOG2E * log_base))
    return saturation, conduct, storage


def lane_lookup(row, index):
    return jnp.take_along_axis(row, index, axis=1, mode="promise_in_bounds")


def conductivity(head, alpha, n1, half_m, ksat):
    power, _, half = powers(head, alpha, n1, half_m)
    root = jnp.exp2(half)
    inner = 1.0 - power * (root * root)
    return (ksat * root) * (inner * inner)


def edge_lanes(values, k, layers, lanes, packed):
    for part, value in enumerate(values):
        at = 2 * (part * layers + k)
        moved = pltpu.roll(value, at + 1, 1)
        packed = jnp.where((lanes == at) | (lanes == at + 1), moved, packed)
    return packed


def edge_rows(refs, row_even_ref, row_odd_ref):
    even = lax.rem(lax.axis_index("bx"), 2) == 0
    for part, ref in enumerate(refs):
        rows = ref.shape[1]
        low = ref[:, 0, :].astype(F32)
        high = ref[:, rows - 1, :].astype(F32)
        row_even_ref[part] = jnp.where(even, high, low)
        row_odd_ref[part] = jnp.where(even, low, high)


def row_halo(own_even, own_odd, row_even, row_odd):
    index = lax.axis_index("bx")
    even = lax.rem(index, 2) == 0
    low = jnp.where(even, row_odd, row_even)
    high = jnp.where(even, row_even, row_odd)
    own_low = jnp.where(even, own_odd, own_even)
    own_high = jnp.where(even, own_even, own_odd)
    low = jnp.where(index == 0, own_low, low)
    high = jnp.where(index == lax.axis_size("bx") - 1, own_high, high)
    return low, high


def lane_halo(own, lane_even, lane_odd):
    index = lax.axis_index("by")
    even = lax.rem(index, 2) == 0
    width = own.shape[1]
    lanes = lax.broadcasted_iota(jnp.int32, own.shape, 1)
    low = jnp.where(even, lane_odd, lane_even)
    high = jnp.where(even, lane_even, lane_odd)
    low = jnp.where(index == 0, pltpu.roll(own, width - 1, 1), low)
    high = jnp.where(index == lax.axis_size("by") - 1, pltpu.roll(own, 1, 1), high)
    return jnp.where(lax.rem(lanes, 2) == 0, low, pltpu.roll(high, width - 2, 1))


def edge_signs(shape):
    x, y = lax.axis_index("bx"), lax.axis_index("by")
    minus = lambda at_edge: jnp.where(at_edge, -1.0, 1.0)
    lanes = lax.broadcasted_iota(jnp.int32, shape, 1)
    return (
        minus(x == 0),
        minus(x == lax.axis_size("bx") - 1),
        jnp.where(
            lax.rem(lanes, 2) == 0, minus(y == 0), minus(y == lax.axis_size("by") - 1)
        ),
    )


def prepare_kernel(
    root_hbm, transp_hbm, infil_hbm, cell_hbm, out_hbm,
    root_ref, transp_ref, infil_ref, cell_ref, out_ref, sems,
):
    peers, fields, per_peer = out_ref.shape
    roots = fields - 2
    steps = prepare_steps(peers)
    count = peers // steps
    span = count * per_peer
    lines = [
        pltpu.make_async_copy(a, b, sems.at[2 * steps + i])
        for i, (a, b) in enumerate(
            [(transp_hbm, transp_ref), (infil_hbm, infil_ref), (cell_hbm, cell_ref)]
        )
    ]
    parts = [
        pltpu.make_async_copy(
            root_hbm.at[:, pl.ds(i * span, span)],
            root_ref.at[:, pl.ds(i * span, span)],
            sems.at[i],
        )
        for i in range(steps)
    ]
    leaves = [
        pltpu.make_async_copy(
            out_ref.at[pl.ds(i * count, count)],
            out_hbm.at[pl.ds(i * count, count)],
            sems.at[steps + i],
        )
        for i in range(steps)
    ]
    for copy in lines + parts:
        copy.start()
    for copy in lines:
        copy.wait()
    for i in range(steps):
        parts[i].wait()
        for peer in range(i * count, (i + 1) * count):
            at = slice(peer * per_peer, (peer + 1) * per_peer)
            out_ref[peer, :roots, :] = root_ref[:, at] * transp_ref[:, at]
            out_ref[peer, roots : roots + 1, :] = infil_ref[:, at]
            out_ref[peer, roots + 1 :, :] = cell_ref[:, at].astype(F32)
        leaves[i].start()
    for copy in leaves:
        copy.wait()


def prepare_steps(peers):
    return 4 if peers % 4 == 0 else 1


def layer_chunks(layers):
    size = 5 if layers % 5 == 0 else layers
    return [(at, size) for at in range(0, layers, size)]


def copies(pairs, sems, layers):
    chunks = layer_chunks(layers)
    return [
        [
            pltpu.make_async_copy(
                a.at[pl.ds(at, size)], b.at[pl.ds(at, size)], sems.at[c * len(pairs) + i]
            )
            for i, (a, b) in enumerate(pairs)
        ]
        for c, (at, size) in enumerate(chunks)
    ]


def edges_kernel(
    h_hbm, soil_hbm, ks_hbm,
    h_ref, soil_ref, ks_ref, row_even_ref, row_odd_ref, lane_ref,
    sems,
):
    layers, rows, width = h_ref.shape
    ins = copies([(h_hbm, h_ref), (soil_hbm, soil_ref), (ks_hbm, ks_ref)], sems, layers)
    for chunk in ins:
        for copy in chunk:
            copy.start()
    lanes = lax.broadcasted_iota(jnp.int32, (rows, width), 1)
    packed = jnp.zeros((rows, width), F32)
    for (at, size), arrive in zip(layer_chunks(layers), ins):
        for copy in arrive:
            copy.wait()
        for k in range(at, at + size):
            packed = edge_lanes(
                (h_ref[k], soil_ref[k].astype(F32), ks_ref[k]), k, layers, lanes, packed
            )
    lane_ref[...] = packed
    edge_rows((h_ref, soil_ref, ks_ref), row_even_ref, row_odd_ref)


def lateral_terms(k, top, size, head_pad, cond_pad, halo_head, halo_cond, lanes):
    width = head_pad.shape[2]
    at = lambda pad, move: pad[k, PAD + top + move : PAD + top + move + size, :]
    head, conduct = at(head_pad, 0), at(cond_pad, 0)
    flow = faces = None
    for move in (-1, 1):
        both = conduct + at(cond_pad, move)
        term = both * (head - at(head_pad, move))
        flow = term if flow is None else flow + term
        faces = both if faces is None else faces + both
    if halo_head is not None:
        halo_head = pltpu.roll(halo_head, (width - 2 * k) % width, 1)
        halo_cond = pltpu.roll(halo_cond, (width - 2 * k) % width, 1)
    for shift, edge in ((1, lanes == 0), (width - 1, lanes == width - 1)):
        other_head = pltpu.roll(head, shift, 1)
        other_cond = pltpu.roll(conduct, shift, 1)
        if halo_head is not None:
            other_head = jnp.where(edge, halo_head, other_head)
            both = conduct + jnp.where(edge, halo_cond, other_cond)
        else:
            both = jnp.where(edge, 0.0, conduct + other_cond)
        flow = flow + both * (head - other_head)
        faces = faces + both
    return head, conduct, flow, faces


VERTICAL = 0.5 / (0.5 * LATERAL)


def first_kernel(
    h_ref, soil_ref, ks_ref, table_ref,
    alpha_hbm, n1_hbm, half_m_hbm, ksat_hbm, room_hbm, sat_hbm, cond_hbm, cond_ref, stor_ref,
    alpha_ref, n1_ref, half_m_ref, ksat_ref, room_ref, sat_ref, sems,
):
    layers, rows, width = h_ref.shape
    outs = copies(
        [
            (alpha_ref, alpha_hbm), (n1_ref, n1_hbm), (half_m_ref, half_m_hbm),
            (ksat_ref, ksat_hbm), (room_ref, room_hbm), (sat_ref, sat_hbm),
            (cond_ref, cond_hbm),
        ],
        sems,
        layers,
    )
    tables = lane_tables(table_ref[...], (8, width))
    for (at, size), leave in zip(layer_chunks(layers), outs):
        for k in range(at, at + size):
            for row in range(0, rows, 8):
                span = slice(row, row + 8)
                kind = soil_ref[k, span, :]
                alpha, n1, half_m, ks3, room = (lane_lookup(t, kind) for t in tables)
                ksat = ks3 * ks_ref[k, span, :]
                alpha_ref[k, span, :] = alpha
                n1_ref[k, span, :] = n1
                half_m_ref[k, span, :] = half_m
                ksat_ref[k, span, :] = ksat
                room_ref[k, span, :] = room
                saturation, conduct, storage = closure(
                    h_ref[k, span, :], alpha, n1, half_m, ksat, room
                )
                sat_ref[k, span, :] = saturation
                cond_ref[k, span, :] = conduct
                stor_ref[k, span, :] = storage
        for copy in leave:
            copy.start()
    for chunk in outs:
        for copy in chunk:
            copy.wait()


def balance_kernel(
    h_ref, cond_ref, stor_ref, table_ref,
    own_even_ref, own_odd_ref, row_even_ref, row_odd_ref,
    res_ref, diag_ref, vert_ref, row_par_ref,
    head_pad, cond_pad,
):
    layers, rows, width = h_ref.shape
    head_pad[:, PAD : PAD + rows, :] = h_ref[...]
    cond_pad[:, PAD : PAD + rows, :] = cond_ref[...]
    sign_low, sign_high, _ = edge_signs((8, width))
    for side, sign in ((0, sign_low), (1, sign_high)):
        head, kind, ks = (
            row_halo(own_even_ref[i], own_odd_ref[i], row_even_ref[i], row_odd_ref[i])[side]
            for i in range(3)
        )
        pars = halo_parameters(table_ref, kind, ks, sign)
        for i in range(4):
            row_par_ref[side, i] = pars[i]
        row = PAD - 1 if side == 0 else PAD + rows
        head_pad[:, row, :] = head
        cond_pad[:, row, :] = conductivity(head, *pars)
    size = HALF if rows % HALF == 0 else rows
    lanes = lax.broadcasted_iota(jnp.int32, (size, width), 1)
    for top in range(0, rows, size):
        span = slice(top, top + size)
        inner = slice(PAD + top, PAD + top + size)
        vert_above = flux_above = None
        for k in range(layers):
            head, conduct, flow, faces = lateral_terms(
                k, top, size, head_pad, cond_pad, None, None, lanes
            )
            diagonal = stor_ref[k, span, :] + faces
            if k < layers - 1:
                vert = VERTICAL * (conduct + cond_pad[k + 1, inner, :])
                flux = vert * (head - head_pad[k + 1, inner, :] + 1.0)
                diagonal = diagonal + vert
                vert_ref[k, span, :] = vert
            else:
                vert = None
                flux = conduct * (2.0 * VERTICAL)
            residual = flux + flow
            if k:
                residual = residual - flux_above
                diagonal = diagonal + vert_above
            res_ref[k, span, :] = residual
            diag_ref[k, span, :] = diagonal
            vert_above, flux_above = vert, flux


def halo_parameters(table_ref, kind, ks, sign):
    pars = [
        lane_lookup(t, jnp.clip(kind.astype(jnp.int32), 0, kind.shape[1] - 1))
        for t in lane_tables(table_ref[...], kind.shape)[:4]
    ]
    return pars[:3] + [sign * (pars[3] * ks)]


def slot_places(ids, width):
    shift = width.bit_length() - 1
    row = ids >> shift
    low = ROW_BLOCK.bit_length() - 1
    return row & (ROW_BLOCK - 1), (row >> low) * width + (ids & (width - 1))


def one_hot(ids, count):
    place = lax.broadcasted_iota(jnp.int32, (count, ids.shape[1]), 0)
    return (place == ids).astype(F32).astype(BF16)


def middle_kernel(
    slots_ref, h_hbm, cond_hbm, alpha_hbm, n1_hbm, half_m_hbm, ksat_hbm, room_hbm, sat_hbm,
    res_ref, diag_ref, vert_ref, table_ref, own_ref, lane_even_ref, lane_odd_ref,
    head_ref, sink_ref, infil_ref, row_even_ref, row_odd_ref, lane_ref,
    alpha_ref, n1_ref, half_m_ref, ksat_ref, room_ref, sat_ref, lane_par_ref,
    total, left_a, left_b, hot_a, hot_b, h_ref, cond_ref, ratio_ref, halo_ref, sems,
):
    layers, rows, width = h_ref.shape
    peers, fields, per_peer = slots_ref.shape
    roots = fields - 2
    values = fields - 1
    blocks = rows // ROW_BLOCK
    half = values * ROW_BLOCK
    group = left_a.shape[1] // per_peer
    steps = peers // group
    loads = [
        pltpu.make_async_copy(a, b, sems.at[i])
        for i, (a, b) in enumerate(
            [
                (h_hbm, h_ref), (cond_hbm, cond_ref), (sat_hbm, sat_ref),
                (alpha_hbm, alpha_ref), (n1_hbm, n1_ref), (half_m_hbm, half_m_ref),
                (ksat_hbm, ksat_ref), (room_hbm, room_ref),
            ]
        )
    ]
    for copy in loads:
        copy.start()
    total[...] = jnp.zeros_like(total)

    def build(step, left, hot):
        for g in range(group):
            block = slots_ref[step * group + g]
            at = slice(g * per_peer, (g + 1) * per_peer)
            row, column = slot_places(block[values : values + 1, :].astype(jnp.int32), width)
            hot[:, at] = one_hot(column, blocks * width)
            mask = lax.broadcasted_iota(jnp.int32, (ROW_BLOCK, per_peer), 0) == row
            high = block.astype(BF16).astype(F32)
            low = block - high
            for f in range(values):
                for base, part in ((0, high), (half, low)):
                    first = base + f * ROW_BLOCK
                    left[first : first + ROW_BLOCK, at] = jnp.where(
                        mask, part[f : f + 1, :], 0.0
                    ).astype(BF16)

    def add(left, hot):
        total[...] += lax.dot_general(
            left[...], hot[...], (((1,), (1,)), ((), ())), preferred_element_type=F32
        )

    build(0, left_a, hot_a)

    def place(pair, carry):
        build(2 * pair + 1, left_b, hot_b)
        add(left_a, hot_a)
        build(jnp.minimum(2 * pair + 2, steps - 1), left_a, hot_a)
        add(left_b, hot_b)
        return carry

    lax.fori_loop(0, steps // 2, place, 0)
    for copy in loads:
        copy.wait()

    def grid(f, b):
        at = f * ROW_BLOCK
        cols = slice(b * width, (b + 1) * width)
        return total[at : at + ROW_BLOCK, cols] + total[half + at : half + at + ROW_BLOCK, cols]

    halo = lane_halo(own_ref[...], lane_even_ref[...], lane_odd_ref[...])
    pars = halo_parameters(
        table_ref,
        pltpu.roll(halo, width - 2 * layers, 1),
        pltpu.roll(halo, width - 4 * layers, 1),
        edge_signs((rows, width))[2],
    )
    for i in range(4):
        lane_par_ref[i] = pars[i]
    halo_ref[0] = halo
    halo_ref[1] = conductivity(halo, *pars)
    lanes = lax.broadcasted_iota(jnp.int32, (ROW_BLOCK, width), 1)
    edge = (lanes == 0) | (lanes == width - 1)
    for b in range(blocks):
        span = slice(b * ROW_BLOCK, (b + 1) * ROW_BLOCK)
        packed = jnp.zeros((ROW_BLOCK, width), F32)
        infil = grid(roots, b)
        infil_ref[span, :] = infil
        value = ratio = None
        for k in range(layers):
            halo_head = pltpu.roll(halo_ref[0, span], (width - 2 * k) % width, 1)
            halo_cond = pltpu.roll(halo_ref[1, span], (width - 2 * k) % width, 1)
            both = jnp.where(edge, cond_ref[k, span, :] + halo_cond, 0.0)
            diagonal = diag_ref[k, span, :] + both
            residual = res_ref[k, span, :] + both * (h_ref[k, span, :] - halo_head)
            if k < roots:
                sink = grid(k, b)
                sink_ref[k, span, :] = sink
                residual = residual + sink
            if k == 0:
                target = infil - residual
            else:
                vert = vert_ref[k - 1, span, :]
                diagonal = diagonal - vert * ratio
                target = vert * value - residual
            inverse = 1.0 / diagonal
            value = target * inverse
            head_ref[k, span, :] = value
            if k < layers - 1:
                ratio = vert_ref[k, span, :] * inverse
                ratio_ref[k, span, :] = ratio
        change = value
        for k in range(layers - 1, -1, -1):
            if k < layers - 1:
                change = head_ref[k, span, :] + ratio_ref[k, span, :] * change
            head = h_ref[k, span, :] + change
            head_ref[k, span, :] = head
            packed = edge_lanes((head,), k, layers, lanes, packed)
        lane_ref[span, :] = packed
    edge_rows((head_ref,), row_even_ref, row_odd_ref)


def close_kernel(
    head_ref, sink_ref, infil_ref,
    alpha_ref, n1_ref, half_m_ref, ksat_ref, room_ref, sat_ref,
    cond_ref, stor_ref, source_ref,
):
    layers, _, _ = head_ref.shape
    roots = sink_ref.shape[0]
    for k in range(layers):
        room = room_ref[k]
        saturation, conduct, storage = closure(
            head_ref[k], alpha_ref[k], n1_ref[k], half_m_ref[k], ksat_ref[k], room
        )
        cond_ref[k] = conduct
        stor_ref[k] = storage
        source = room * (saturation - sat_ref[k])
        if k < roots:
            source = source + sink_ref[k]
        if k == 0:
            source = source - infil_ref[...]
        source_ref[k] = source


def last_kernel(
    slots_ref, old_head_ref, cond_ref, stor_ref, source_ref, sink_ref,
    alpha_ref, n1_ref, half_m_ref, row_par_ref, lane_par_ref,
    own_even_ref, own_odd_ref, row_even_ref, row_odd_ref, own_ref, lane_even_ref, lane_odd_ref,
    head_hbm, reply_ref,
    head_pad, cond_pad, head_ref, ratio_ref, value_ref, halo_ref, stress_ref, sems,
):
    layers, rows, width = head_ref.shape
    peers, fields, per_peer = slots_ref.shape
    roots = fields - 2
    blocks = rows // ROW_BLOCK
    head_pad[:, PAD : PAD + rows, :] = old_head_ref[...]
    cond_pad[:, PAD : PAD + rows, :] = cond_ref[...]
    sides = row_halo(own_even_ref[0], own_odd_ref[0], row_even_ref[0], row_odd_ref[0])
    for side, row in ((0, PAD - 1), (1, PAD + rows)):
        head_pad[:, row, :] = sides[side]
        pars = [row_par_ref[side, i] for i in range(4)]
        cond_pad[:, row, :] = conductivity(sides[side], *pars)
    halo = lane_halo(own_ref[...], lane_even_ref[...], lane_odd_ref[...])
    halo_ref[0] = halo
    halo_ref[1] = conductivity(halo, *(lane_par_ref[i] for i in range(4)))
    size = HALF if rows % HALF == 0 else rows
    lanes = lax.broadcasted_iota(jnp.int32, (size, width), 1)
    for top in range(0, rows, size):
        span = slice(top, top + size)
        vert_above = flux_above = ratio_above = value = None
        for k in range(layers):
            head, conduct, flow, faces = lateral_terms(
                k, top, size, head_pad, cond_pad, halo_ref[0, span], halo_ref[1, span], lanes
            )
            diagonal = stor_ref[k, span, :] + faces
            if k < layers - 1:
                vert = VERTICAL * (conduct + cond_ref[k + 1, span, :])
                flux = vert * (head - old_head_ref[k + 1, span, :] + 1.0)
                diagonal = diagonal + vert
            else:
                vert = None
                flux = conduct * (2.0 * VERTICAL)
            residual = flux + flow + source_ref[k, span, :]
            if k:
                residual = residual - flux_above
                diagonal = diagonal + vert_above
                diagonal = diagonal - vert_above * ratio_above
                inverse = 1.0 / diagonal
                value = (vert_above * value - residual) * inverse
            else:
                inverse = 1.0 / diagonal
                value = -residual * inverse
            value_ref[k, span, :] = value
            if vert is not None:
                ratio_above = vert * inverse
                ratio_ref[k, span, :] = ratio_above
            vert_above, flux_above = vert, flux
        change = value
        head_ref[layers - 1, span, :] = old_head_ref[layers - 1, span, :] + change
        numer = denom = None
        for k in range(layers - 2, -1, -1):
            change = value_ref[k, span, :] + ratio_ref[k, span, :] * change
            head = old_head_ref[k, span, :] + change
            head_ref[k, span, :] = head
            if k < roots:
                half = powers(
                    head, alpha_ref[k, span, :], n1_ref[k, span, :], half_m_ref[k, span, :]
                )[2]
                sink = sink_ref[k, span, :]
                term = sink * jnp.exp2(half + half)
                numer = term if numer is None else numer + term
                denom = sink if denom is None else denom + sink
        held = denom > 0.0
        stress_ref[span, :] = jnp.where(held, numer / jnp.where(held, denom, 1.0), 0.0)
    leave = pltpu.make_async_copy(head_ref, head_hbm, sems.at[0])
    leave.start()
    wide = jnp.concatenate(
        [stress_ref[b * ROW_BLOCK : (b + 1) * ROW_BLOCK, :] for b in range(blocks)], 1
    )
    high = wide.astype(BF16)
    both = jnp.concatenate([high, (wide - high.astype(F32)).astype(BF16)], 0)

    def answer(block, carry):
        for g in range(UNROLL):
            peer = block * UNROLL + g
            ids = slots_ref[peer, fields - 1 : fields, :].astype(jnp.int32)
            row, column = slot_places(ids, width)
            hot = one_hot(column, blocks * width)
            found = jnp.dot(both, hot, preferred_element_type=F32)
            found = found[:ROW_BLOCK] + found[ROW_BLOCK:]
            mask = lax.broadcasted_iota(jnp.int32, (ROW_BLOCK, per_peer), 0) == row
            reply_ref[peer] = jnp.sum(jnp.where(mask, found, 0.0), 0, keepdims=True)
        return carry

    lax.fori_loop(0, peers // UNROLL, answer, 0)
    leave.wait()


def swaps():
    count_x, count_y = lax.axis_size("bx"), lax.axis_size("by")

    def pairs(partner):
        return [
            (x * count_y + y, px * count_y + py)
            for x in range(count_x)
            for y in range(count_y)
            for px, py in [partner(x, y)]
        ]

    odd = lambda i: i + 1 if i % 2 else i - 1
    return (
        pairs(lambda x, y: (x ^ 1, y)),
        pairs(lambda x, y: (odd(x) % count_x, y)),
        pairs(lambda x, y: (x, y ^ 1)),
        pairs(lambda x, y: (x, odd(y)) if 0 < y < count_y - 1 else (x ^ 1, y)),
    )


def exchange(row_even, row_odd, packed):
    even_x, odd_x, even_y, odd_y = swaps()
    axes = ("bx", "by")

    def send(message, pairs):
        return lax.ppermute(message, axes, pairs)

    return (
        row_even,
        row_odd,
        send(row_even, even_x),
        send(row_odd, odd_x),
        packed,
        send(packed, even_y),
        send(packed, odd_y),
    )


def call(kernel, ins, outs, scratch, limit=20, flops=0):
    return pl.pallas_call(
        kernel,
        in_specs=[pl.BlockSpec(memory_space=m) for m in ins],
        out_specs=[pl.BlockSpec(memory_space=m) for _, _, m in outs],
        out_shape=[HBM(s, t) if m is HBM else jax.ShapeDtypeStruct(s, t) for s, t, m in outs],
        scratch_shapes=scratch,
        cost_estimate=pl.CostEstimate(flops=flops, bytes_accessed=flops, transcendentals=0),
        compiler_params=pltpu.CompilerParams(vmem_limit_bytes=limit * MIB),
    )


def in_hbm(*arrays):
    return [pltpu.with_memory_space_constraint(a, HBM) for a in arrays]


def prepare(root_fraction, transpiration, infiltration, clump_cell, peers, per_peer):
    roots, slot_count = root_fraction.shape
    line = (1, slot_count)
    return pl.pallas_call(
        prepare_kernel,
        in_specs=[pl.BlockSpec(memory_space=HBM)] * 4,
        out_specs=pl.BlockSpec(memory_space=HBM),
        out_shape=HBM((peers, roots + 2, per_peer), F32),
        scratch_shapes=[
            VMEM(root_fraction.shape, F32), VMEM(line, F32), VMEM(line, F32),
            VMEM(line, jnp.int32), VMEM((peers, roots + 2, per_peer), F32),
            pltpu.SemaphoreType.DMA((2 * prepare_steps(peers) + 3,)),
        ],
        name="prepare",
        compiler_params=pltpu.CompilerParams(vmem_limit_bytes=6 * MIB),
    )(*in_hbm(root_fraction, transpiration[None], infiltration[None], clump_cell[None]))


def on_device(
    h_old,
    soil_type,
    ks_scale,
    soil_table,
    clump_brick,
    clump_cell,
    root_fraction,
    transpiration,
    infiltration,
):
    layers, rows, width = h_old.shape
    peers = lax.axis_size("bx") * lax.axis_size("by")
    roots, slot_count = root_fraction.shape
    per_peer = slot_count // peers
    cells = (layers, rows, width)
    lane_msg = (rows, width)
    axes = ("bx", "by")
    on_chip = lambda *shapes: [(s, F32, VMEM) for s in shapes]
    in_main = lambda *shapes: [(s, F32, HBM) for s in shapes]
    buffers = lambda n: [VMEM(cells, F32)] * n
    semaphores = pltpu.SemaphoreType.DMA
    chunks = len(layer_chunks(layers))

    slots = lax.all_to_all(
        prepare(root_fraction, transpiration, infiltration, clump_cell, peers, per_peer),
        axes,
        split_axis=0,
        concat_axis=0,
        tiled=True,
    )
    table = jnp.pad(soil_table, ((0, 0), (0, width - soil_table.shape[1])))
    raw_msg = (3, layers, width)
    head, soil, scale, row_even, row_odd, packed = call(
        edges_kernel,
        [HBM] * 3,
        on_chip(cells) + [(cells, jnp.int32, VMEM)] + on_chip(cells, raw_msg, raw_msg, lane_msg),
        [semaphores((3 * chunks,))],
    )(*in_hbm(h_old, soil_type, ks_scale))
    pads = [VMEM((layers, rows + 2 * PAD, width), F32)] * 2
    halo = [VMEM((2,) + lane_msg, F32)]
    arrived = exchange(row_even, row_odd, packed)
    alpha, n1, half_m, ksat, room, old_sat, stored, conduct, storage = call(
        first_kernel,
        [VMEM] * 4,
        in_main(*[cells] * 7) + on_chip(*[cells] * 2),
        buffers(6) + [semaphores((7 * chunks,))],
        flops=8_000_000,
    )(head, soil, scale, table)
    own_even, own_odd, row_even, row_odd, own, lane_even, lane_odd = arrived
    residual, diagonal, vert, row_par = call(
        balance_kernel,
        [VMEM] * 8,
        on_chip(*[cells] * 3, (2, 4, layers, width)),
        pads,
        flops=4_000_000,
    )(head, conduct, storage, table, own_even, own_odd, row_even, row_odd)
    values = roots + 1
    columns = rows // ROW_BLOCK * width
    group = GROUP if peers % (2 * GROUP) == 0 else 1
    lefts = [VMEM((2 * values * ROW_BLOCK, group * per_peer), BF16)] * 2
    hots = [VMEM((columns, group * per_peer), BF16)] * 2
    row_msg = (1, layers, width)
    (
        head, sink, infil, row_even, row_odd, packed,
        alpha, n1, half_m, ksat, room, old_sat, lane_par,
    ) = call(
        middle_kernel,
        [VMEM] + [HBM] * 8 + [VMEM] * 7,
        on_chip(cells, (roots, rows, width), lane_msg, row_msg, row_msg, lane_msg)
        + on_chip(*[cells] * 6, (4,) + lane_msg),
        [VMEM((2 * values * ROW_BLOCK, columns), F32)] + lefts + hots
        + buffers(3) + halo + [semaphores((8,))],
    )(
        slots, *in_hbm(h_old, stored, alpha, n1, half_m, ksat, room, old_sat),
        residual, diagonal, vert, table, own, lane_even, lane_odd,
    )
    arrived = exchange(row_even, row_odd, packed)
    conduct, storage, source = call(
        close_kernel, [VMEM] * 9, on_chip(*[cells] * 3), [], limit=4, flops=4_000_000
    )(head, sink, infil, alpha, n1, half_m, ksat, room, old_sat)
    head, reply = call(
        last_kernel,
        [VMEM] * 18,
        in_main(cells) + on_chip((peers, 1, per_peer)),
        pads + buffers(3) + halo + [VMEM(lane_msg, F32), semaphores((1,))],
    )(
        slots, head, conduct, storage, source, sink, alpha, n1, half_m, row_par, lane_par,
        *arrived,
    )
    stress = lax.all_to_all(reply, axes, split_axis=0, concat_axis=0, tiled=True)
    return head, stress.reshape(slot_count)


def solution(mesh):
    placed = (
        P(None, "bx", "by"),
        P(None, "bx", "by"),
        P(None, "bx", "by"),
        P(),
        P(("bx", "by")),
        P(("bx", "by")),
        P(None, ("bx", "by")),
        P(("bx", "by")),
        P(("bx", "by")),
    )
    return jax.shard_map(
        on_device,
        mesh=mesh,
        in_specs=placed,
        out_specs=(P(None, "bx", "by"), P(("bx", "by"))),
        check_vma=False,
    )
```

```python
import jax
import jax.numpy as jnp
from jax import lax
from jax.experimental import pallas as pl
from jax.experimental.pallas import tpu as pltpu
from jax.sharding import PartitionSpec as P


RESIDUAL_WATER = 0.05
STORAGE = 0.2
TIME_STEP = 0.5
LATERAL = 0.5
TINY = 1e-30
ROW_BLOCK = 32
HALF = 32
LAST = 64
UNROLL = 8
GROUP = 4
LOG2E = 1.4426950408889634
PAD = 8
F32 = jnp.float32
BF16 = jnp.bfloat16
MIB = 1 << 20
VMEM = pltpu.VMEM
HBM = pltpu.HBM


def lane_tables(table, shape):
    t0, t1, t2, t3 = (table[i : i + 1, :] for i in range(4))
    alpha = 4.0 * t0
    n1 = 0.2 + 2.0 * t1
    half_m = 0.5 * n1 / (1.0 + n1)
    ks3 = (0.5 * LATERAL * 3.0) * t2
    room = ((0.3 - RESIDUAL_WATER) + 0.3 * t3) * (1.0 / TIME_STEP)
    rows = (alpha, LOG2E * n1, -LOG2E * half_m, ks3, room)
    return [jnp.broadcast_to(r, shape) for r in rows]


def powers(head, alpha, n1, half_m):
    suction = jnp.maximum(alpha * jnp.maximum(-head, 0.0), TINY)
    power = jnp.exp2(n1 * lax.log(suction))
    log_base = lax.log(1.0 + suction * power)
    return power, log_base, half_m * log_base


def closure(head, alpha, n1, half_m, ksat, room):
    power, log_base, half = powers(head, alpha, n1, half_m)
    root = jnp.exp2(half)
    saturation = root * root
    share = power * saturation
    inner = 1.0 - share
    conduct = (ksat * root) * (inner * inner)
    cap = (room * (1.0 / LOG2E)) * (n1 * alpha)
    storage = STORAGE / TIME_STEP + cap * (share * jnp.exp2(-LOG2E * log_base))
    return saturation, conduct, storage


def lane_lookup(row, index):
    return jnp.take_along_axis(row, index, axis=1, mode="promise_in_bounds")


def conductivity(head, alpha, n1, half_m, ksat):
    power, _, half = powers(head, alpha, n1, half_m)
    root = jnp.exp2(half)
    inner = 1.0 - power * (root * root)
    return (ksat * root) * (inner * inner)


def edge_lanes(values, k, layers, lanes, packed):
    for part, value in enumerate(values):
        at = 2 * (part * layers + k)
        moved = pltpu.roll(value, at + 1, 1)
        packed = jnp.where((lanes == at) | (lanes == at + 1), moved, packed)
    return packed


def edge_rows(refs, row_even_ref, row_odd_ref):
    even = lax.rem(lax.axis_index("bx"), 2) == 0
    for part, ref in enumerate(refs):
        rows = ref.shape[1]
        low = ref[:, 0, :].astype(F32)
        high = ref[:, rows - 1, :].astype(F32)
        row_even_ref[part] = jnp.where(even, high, low)
        row_odd_ref[part] = jnp.where(even, low, high)


def row_halo(own_even, own_odd, row_even, row_odd):
    index = lax.axis_index("bx")
    even = lax.rem(index, 2) == 0
    low = jnp.where(even, row_odd, row_even)
    high = jnp.where(even, row_even, row_odd)
    own_low = jnp.where(even, own_odd, own_even)
    own_high = jnp.where(even, own_even, own_odd)
    low = jnp.where(index == 0, own_low, low)
    high = jnp.where(index == lax.axis_size("bx") - 1, own_high, high)
    return low, high


def lane_halo(own, lane_even, lane_odd):
    index = lax.axis_index("by")
    even = lax.rem(index, 2) == 0
    width = own.shape[1]
    lanes = lax.broadcasted_iota(jnp.int32, own.shape, 1)
    low = jnp.where(even, lane_odd, lane_even)
    high = jnp.where(even, lane_even, lane_odd)
    low = jnp.where(index == 0, pltpu.roll(own, width - 1, 1), low)
    high = jnp.where(index == lax.axis_size("by") - 1, pltpu.roll(own, 1, 1), high)
    return jnp.where(lax.rem(lanes, 2) == 0, low, pltpu.roll(high, width - 2, 1))


def edge_signs(shape):
    x, y = lax.axis_index("bx"), lax.axis_index("by")
    minus = lambda at_edge: jnp.where(at_edge, -1.0, 1.0)
    lanes = lax.broadcasted_iota(jnp.int32, shape, 1)
    return (
        minus(x == 0),
        minus(x == lax.axis_size("bx") - 1),
        jnp.where(
            lax.rem(lanes, 2) == 0, minus(y == 0), minus(y == lax.axis_size("by") - 1)
        ),
    )


def prepare_kernel(
    root_hbm, transp_hbm, infil_hbm, cell_hbm, out_hbm,
    root_ref, transp_ref, infil_ref, cell_ref, out_ref, sems,
):
    peers, fields, per_peer = out_ref.shape
    roots = fields - 2
    steps = prepare_steps(peers)
    count = peers // steps
    span = count * per_peer
    lines = [
        pltpu.make_async_copy(a, b, sems.at[2 * steps + i])
        for i, (a, b) in enumerate(
            [(transp_hbm, transp_ref), (infil_hbm, infil_ref), (cell_hbm, cell_ref)]
        )
    ]
    parts = [
        pltpu.make_async_copy(
            root_hbm.at[:, pl.ds(i * span, span)],
            root_ref.at[:, pl.ds(i * span, span)],
            sems.at[i],
        )
        for i in range(steps)
    ]
    leaves = [
        pltpu.make_async_copy(
            out_ref.at[pl.ds(i * count, count)],
            out_hbm.at[pl.ds(i * count, count)],
            sems.at[steps + i],
        )
        for i in range(steps)
    ]
    for copy in lines + parts:
        copy.start()
    for copy in lines:
        copy.wait()
    for i in range(steps):
        parts[i].wait()
        for peer in range(i * count, (i + 1) * count):
            at = slice(peer * per_peer, (peer + 1) * per_peer)
            out_ref[peer, :roots, :] = root_ref[:, at] * transp_ref[:, at]
            out_ref[peer, roots : roots + 1, :] = infil_ref[:, at]
            out_ref[peer, roots + 1 :, :] = cell_ref[:, at].astype(F32)
        leaves[i].start()
    for copy in leaves:
        copy.wait()


def prepare_steps(peers):
    return 4 if peers % 4 == 0 else 1


def layer_chunks(layers):
    size = 5 if layers % 5 == 0 else layers
    return [(at, size) for at in range(0, layers, size)]


def copies(pairs, sems, layers):
    chunks = layer_chunks(layers)
    return [
        [
            pltpu.make_async_copy(
                a.at[pl.ds(at, size)], b.at[pl.ds(at, size)], sems.at[c * len(pairs) + i]
            )
            for i, (a, b) in enumerate(pairs)
        ]
        for c, (at, size) in enumerate(chunks)
    ]


def edges_kernel(
    h_hbm, soil_hbm, ks_hbm,
    h_ref, soil_ref, ks_ref, row_even_ref, row_odd_ref, lane_ref,
    sems,
):
    layers, rows, width = h_ref.shape
    ins = copies([(h_hbm, h_ref), (soil_hbm, soil_ref), (ks_hbm, ks_ref)], sems, layers)
    for chunk in ins:
        for copy in chunk:
            copy.start()
    lanes = lax.broadcasted_iota(jnp.int32, (rows, width), 1)
    packed = jnp.zeros((rows, width), F32)
    for (at, size), arrive in zip(layer_chunks(layers), ins):
        for copy in arrive:
            copy.wait()
        for k in range(at, at + size):
            packed = edge_lanes(
                (h_ref[k], soil_ref[k].astype(F32), ks_ref[k]), k, layers, lanes, packed
            )
    lane_ref[...] = packed
    edge_rows((h_ref, soil_ref, ks_ref), row_even_ref, row_odd_ref)


def lateral_terms(k, top, size, head_pad, cond_pad, lanes):
    width = head_pad.shape[2]
    at = lambda pad, move: pad[k, PAD + top + move : PAD + top + move + size, :]
    head, conduct = at(head_pad, 0), at(cond_pad, 0)
    flow = faces = None
    for move in (-1, 1):
        both = conduct + at(cond_pad, move)
        term = both * (head - at(head_pad, move))
        flow = term if flow is None else flow + term
        faces = both if faces is None else faces + both
    for shift, edge in ((1, lanes == 0), (width - 1, lanes == width - 1)):
        both = jnp.where(edge, 0.0, conduct + pltpu.roll(conduct, shift, 1))
        flow = flow + both * (head - pltpu.roll(head, shift, 1))
        faces = faces + both
    return head, conduct, flow, faces


VERTICAL = 0.5 / (0.5 * LATERAL)


def first_kernel(
    h_ref, soil_ref, ks_ref, table_ref,
    alpha_hbm, n1_hbm, half_m_hbm, ksat_hbm, room_hbm, sat_hbm, cond_hbm, cond_ref, stor_ref,
    alpha_ref, n1_ref, half_m_ref, ksat_ref, room_ref, sat_ref, sems,
):
    layers, rows, width = h_ref.shape
    outs = copies(
        [
            (alpha_ref, alpha_hbm), (n1_ref, n1_hbm), (half_m_ref, half_m_hbm),
            (ksat_ref, ksat_hbm), (room_ref, room_hbm), (sat_ref, sat_hbm),
            (cond_ref, cond_hbm),
        ],
        sems,
        layers,
    )
    tables = lane_tables(table_ref[...], (8, width))
    for (at, size), leave in zip(layer_chunks(layers), outs):
        for k in range(at, at + size):
            for row in range(0, rows, 8):
                span = slice(row, row + 8)
                kind = soil_ref[k, span, :]
                alpha, n1, half_m, ks3, room = (lane_lookup(t, kind) for t in tables)
                ksat = ks3 * ks_ref[k, span, :]
                alpha_ref[k, span, :] = alpha
                n1_ref[k, span, :] = n1
                half_m_ref[k, span, :] = half_m
                ksat_ref[k, span, :] = ksat
                room_ref[k, span, :] = room
                saturation, conduct, storage = closure(
                    h_ref[k, span, :], alpha, n1, half_m, ksat, room
                )
                sat_ref[k, span, :] = saturation
                cond_ref[k, span, :] = conduct
                stor_ref[k, span, :] = storage
        for copy in leave:
            copy.start()
    for chunk in outs:
        for copy in chunk:
            copy.wait()


def balance_kernel(
    h_ref, cond_ref, stor_ref, table_ref,
    own_even_ref, own_odd_ref, row_even_ref, row_odd_ref,
    res_ref, diag_ref, vert_ref, row_par_ref,
    head_pad, cond_pad,
):
    _, rows, width = h_ref.shape
    head_pad[:, PAD : PAD + rows, :] = h_ref[...]
    cond_pad[:, PAD : PAD + rows, :] = cond_ref[...]
    sign_low, sign_high, _ = edge_signs((8, width))
    for side, sign in ((0, sign_low), (1, sign_high)):
        head, kind, ks = (
            row_halo(own_even_ref[i], own_odd_ref[i], row_even_ref[i], row_odd_ref[i])[side]
            for i in range(3)
        )
        pars = halo_parameters(table_ref, kind, ks, sign)
        for i in range(4):
            row_par_ref[side, i] = pars[i]
        row = PAD - 1 if side == 0 else PAD + rows
        head_pad[:, row, :] = head
        cond_pad[:, row, :] = conductivity(head, *pars)
    interior(head_pad, cond_pad, stor_ref, None, res_ref, diag_ref, vert_ref)


def interior(head_pad, cond_pad, stor_ref, source_ref, res_ref, diag_ref, vert_ref):
    layers, rows, width = res_ref.shape
    size = HALF if rows % HALF == 0 else rows
    lanes = lax.broadcasted_iota(jnp.int32, (size, width), 1)
    for top in range(0, rows, size):
        span = slice(top, top + size)
        inner = slice(PAD + top, PAD + top + size)
        vert_above = flux_above = None
        for k in range(layers):
            head, conduct, flow, faces = lateral_terms(k, top, size, head_pad, cond_pad, lanes)
            diagonal = stor_ref[k, span, :] + faces
            if k < layers - 1:
                vert = VERTICAL * (conduct + cond_pad[k + 1, inner, :])
                flux = vert * (head - head_pad[k + 1, inner, :] + 1.0)
                diagonal = diagonal + vert
                vert_ref[k, span, :] = vert
            else:
                vert = None
                flux = conduct * (2.0 * VERTICAL)
            residual = flux + flow
            if source_ref is not None:
                residual = residual + source_ref[k, span, :]
            if k:
                residual = residual - flux_above
                diagonal = diagonal + vert_above
            res_ref[k, span, :] = residual
            diag_ref[k, span, :] = diagonal
            vert_above, flux_above = vert, flux


def halo_parameters(table_ref, kind, ks, sign):
    pars = [
        lane_lookup(t, jnp.clip(kind.astype(jnp.int32), 0, kind.shape[1] - 1))
        for t in lane_tables(table_ref[...], kind.shape)[:4]
    ]
    return pars[:3] + [sign * (pars[3] * ks)]


def add_rows(array, part, row):
    pieces = [array[:row], array[row : row + 8] + part, array[row + 8 :]]
    return jnp.concatenate([p for p in pieces if p.shape[0]], 0)


def slot_places(ids, width):
    shift = width.bit_length() - 1
    row = ids >> shift
    low = ROW_BLOCK.bit_length() - 1
    return row & (ROW_BLOCK - 1), (row >> low) * width + (ids & (width - 1))


def one_hot(ids, count):
    place = lax.broadcasted_iota(jnp.int32, (count, ids.shape[1]), 0)
    return (place == ids).astype(F32).astype(BF16)


def middle_kernel(
    slots_ref, h_hbm, cond_hbm, alpha_hbm, n1_hbm, half_m_hbm, ksat_hbm, room_hbm, sat_hbm,
    res_ref, diag_ref, vert_ref, table_ref, own_ref, lane_even_ref, lane_odd_ref,
    head_ref, sink_ref, infil_ref, row_even_ref, row_odd_ref, lane_ref,
    alpha_ref, n1_ref, half_m_ref, ksat_ref, room_ref, sat_ref, lane_par_ref,
    total, left_a, left_b, hot_a, hot_b, h_ref, cond_ref, ratio_ref, halo_ref, sems,
):
    layers, rows, width = h_ref.shape
    peers, fields, per_peer = slots_ref.shape
    roots = fields - 2
    values = fields - 1
    blocks = rows // ROW_BLOCK
    half = values * ROW_BLOCK
    group = left_a.shape[1] // per_peer
    steps = peers // group
    loads = [
        pltpu.make_async_copy(a, b, sems.at[i])
        for i, (a, b) in enumerate(
            [
                (h_hbm, h_ref), (cond_hbm, cond_ref), (sat_hbm, sat_ref),
                (alpha_hbm, alpha_ref), (n1_hbm, n1_ref), (half_m_hbm, half_m_ref),
                (ksat_hbm, ksat_ref), (room_hbm, room_ref),
            ]
        )
    ]
    for copy in loads:
        copy.start()
    total[...] = jnp.zeros_like(total)

    def build(step, left, hot):
        for g in range(group):
            block = slots_ref[step * group + g]
            at = slice(g * per_peer, (g + 1) * per_peer)
            row, column = slot_places(block[values : values + 1, :].astype(jnp.int32), width)
            hot[:, at] = one_hot(column, blocks * width)
            mask = lax.broadcasted_iota(jnp.int32, (ROW_BLOCK, per_peer), 0) == row
            high = block.astype(BF16).astype(F32)
            low = block - high
            for f in range(values):
                for base, part in ((0, high), (half, low)):
                    first = base + f * ROW_BLOCK
                    left[first : first + ROW_BLOCK, at] = jnp.where(
                        mask, part[f : f + 1, :], 0.0
                    ).astype(BF16)

    def add(left, hot):
        total[...] += lax.dot_general(
            left[...], hot[...], (((1,), (1,)), ((), ())), preferred_element_type=F32
        )

    build(0, left_a, hot_a)

    def place(pair, carry):
        build(2 * pair + 1, left_b, hot_b)
        add(left_a, hot_a)
        build(jnp.minimum(2 * pair + 2, steps - 1), left_a, hot_a)
        add(left_b, hot_b)
        return carry

    lax.fori_loop(0, steps // 2, place, 0)
    for copy in loads:
        copy.wait()

    def grid(f, b):
        at = f * ROW_BLOCK
        cols = slice(b * width, (b + 1) * width)
        return total[at : at + ROW_BLOCK, cols] + total[half + at : half + at + ROW_BLOCK, cols]

    halo = lane_halo(own_ref[...], lane_even_ref[...], lane_odd_ref[...])
    pars = halo_parameters(
        table_ref,
        pltpu.roll(halo, width - 2 * layers, 1),
        pltpu.roll(halo, width - 4 * layers, 1),
        edge_signs((rows, width))[2],
    )
    for i in range(4):
        lane_par_ref[i] = pars[i]
    halo_ref[0] = halo
    halo_ref[1] = conductivity(halo, *pars)
    lanes = lax.broadcasted_iota(jnp.int32, (rows, width), 1)
    edge = (lanes == 0) | (lanes == width - 1)
    whole = lambda f: jnp.concatenate([grid(f, b) for b in range(blocks)], 0)
    infil = whole(roots)
    infil_ref[...] = infil
    value = ratio = None
    for k in range(layers):
        halo_head = pltpu.roll(halo_ref[0], (width - 2 * k) % width, 1)
        halo_cond = pltpu.roll(halo_ref[1], (width - 2 * k) % width, 1)
        both = jnp.where(edge, cond_ref[k] + halo_cond, 0.0)
        diagonal = diag_ref[k] + both
        residual = res_ref[k] + both * (h_ref[k] - halo_head)
        if k < roots:
            sink = whole(k)
            sink_ref[k] = sink
            residual = residual + sink
        if k == 0:
            target = infil - residual
        else:
            vert = vert_ref[k - 1]
            diagonal = diagonal - vert * ratio
            target = vert * value - residual
        inverse = 1.0 / diagonal
        value = target * inverse
        head_ref[k] = value
        if k < layers - 1:
            ratio = vert_ref[k] * inverse
            ratio_ref[k] = ratio
    change = value
    packed = jnp.zeros((rows, width), F32)
    for k in range(layers - 1, -1, -1):
        if k < layers - 1:
            change = head_ref[k] + ratio_ref[k] * change
        head = h_ref[k] + change
        head_ref[k] = head
        packed = edge_lanes((head,), k, layers, lanes, packed)
    lane_ref[...] = packed
    edge_rows((head_ref,), row_even_ref, row_odd_ref)


def close_kernel(
    head_ref, sink_ref, infil_ref,
    alpha_ref, n1_ref, half_m_ref, ksat_ref, room_ref, sat_ref,
    cond_ref, res_ref, diag_ref, vert_ref, denom_ref,
    head_pad, cond_pad, stor_ref, source_ref,
):
    layers, rows, _ = head_ref.shape
    roots = sink_ref.shape[0]
    denom = None
    for k in range(layers):
        room = room_ref[k]
        head = head_ref[k]
        saturation, conduct, storage = closure(
            head, alpha_ref[k], n1_ref[k], half_m_ref[k], ksat_ref[k], room
        )
        cond_ref[k] = conduct
        head_pad[k, PAD : PAD + rows, :] = head
        cond_pad[k, PAD : PAD + rows, :] = conduct
        for row, beyond in ((0, PAD - 1), (rows - 1, PAD + rows)):
            head_pad[k, beyond : beyond + 1, :] = head[row : row + 1]
            cond_pad[k, beyond : beyond + 1, :] = -conduct[row : row + 1]
        stor_ref[k] = storage
        source = room * (saturation - sat_ref[k])
        if k < roots:
            sink = sink_ref[k]
            source = source + sink
            denom = sink if denom is None else denom + sink
        if k == 0:
            source = source - infil_ref[...]
        source_ref[k] = source
    denom_ref[...] = denom
    interior(head_pad, cond_pad, stor_ref, source_ref, res_ref, diag_ref, vert_ref)


def last_kernel(
    slots_ref, old_head_ref, cond_ref, old_res_ref, old_diag_ref, vert_ref, denom_ref, sink_ref,
    alpha_ref, n1_ref, half_m_ref, row_par_ref, lane_par_ref,
    own_even_ref, own_odd_ref, row_even_ref, row_odd_ref, own_ref, lane_even_ref, lane_odd_ref,
    head_hbm, reply_ref,
    head_ref, ratio_ref, value_ref, halo_ref, side_ref, stress_ref, sems,
):
    layers, rows, width = head_ref.shape
    peers, fields, per_peer = slots_ref.shape
    roots = fields - 2
    blocks = rows // ROW_BLOCK
    sides = row_halo(own_even_ref[0], own_odd_ref[0], row_even_ref[0], row_odd_ref[0])
    for side in range(2):
        side_ref[side, 0] = sides[side]
        side_ref[side, 1] = conductivity(sides[side], *(row_par_ref[side, i] for i in range(4)))
    halo = lane_halo(own_ref[...], lane_even_ref[...], lane_odd_ref[...])
    halo_ref[0] = halo
    halo_ref[1] = conductivity(halo, *(lane_par_ref[i] for i in range(4)))
    size = LAST if rows % LAST == 0 else rows
    lanes = lax.broadcasted_iota(jnp.int32, (size, width), 1)
    edge = (lanes == 0) | (lanes == width - 1)
    places = lax.broadcasted_iota(jnp.int32, (8, width), 0)
    for top in range(0, rows, size):
        span = slice(top, top + size)
        value = ratio = None
        for k in range(layers):
            head, conduct = old_head_ref[k, span, :], cond_ref[k, span, :]
            halo_head = pltpu.roll(halo_ref[0, span], (width - 2 * k) % width, 1)
            halo_cond = pltpu.roll(halo_ref[1, span], (width - 2 * k) % width, 1)
            both = jnp.where(edge, conduct + halo_cond, 0.0)
            faces = both
            flow = both * (head - halo_head)
            for side, row, holds in (
                (0, 0, top == 0), (1, size - 8, top + size == rows)
            ):
                if holds:
                    part = slice(row, row + 8)
                    both = jnp.where(
                        places == (0 if side == 0 else 7),
                        conduct[part] + side_ref[side, 1, k : k + 1, :],
                        0.0,
                    )
                    more = both * (head[part] - side_ref[side, 0, k : k + 1, :])
                    faces = add_rows(faces, both, row)
                    flow = add_rows(flow, more, row)
            diagonal = old_diag_ref[k, span, :] + faces
            residual = old_res_ref[k, span, :] + flow
            if k:
                vert = vert_ref[k - 1, span, :]
                diagonal = diagonal - vert * ratio
                target = vert * value - residual
            else:
                target = -residual
            inverse = 1.0 / diagonal
            value = target * inverse
            value_ref[k, span, :] = value
            if k < layers - 1:
                ratio = vert_ref[k, span, :] * inverse
                ratio_ref[k, span, :] = ratio
        change = value
        head_ref[layers - 1, span, :] = old_head_ref[layers - 1, span, :] + change
        numer = None
        for k in range(layers - 2, -1, -1):
            change = value_ref[k, span, :] + ratio_ref[k, span, :] * change
            head = old_head_ref[k, span, :] + change
            head_ref[k, span, :] = head
            if k < roots:
                half = powers(
                    head, alpha_ref[k, span, :], n1_ref[k, span, :], half_m_ref[k, span, :]
                )[2]
                term = sink_ref[k, span, :] * jnp.exp2(half + half)
                numer = term if numer is None else numer + term
        denom = denom_ref[span, :]
        held = denom > 0.0
        stress_ref[span, :] = jnp.where(held, numer / jnp.where(held, denom, 1.0), 0.0)
    leave = pltpu.make_async_copy(head_ref, head_hbm, sems.at[0])
    leave.start()
    wide = jnp.concatenate(
        [stress_ref[b * ROW_BLOCK : (b + 1) * ROW_BLOCK, :] for b in range(blocks)], 1
    )
    high = wide.astype(BF16)
    both = jnp.concatenate([high, (wide - high.astype(F32)).astype(BF16)], 0)

    def answer(block, carry):
        for g in range(UNROLL):
            peer = block * UNROLL + g
            ids = slots_ref[peer, fields - 1 : fields, :].astype(jnp.int32)
            row, column = slot_places(ids, width)
            hot = one_hot(column, blocks * width)
            found = jnp.dot(both, hot, preferred_element_type=F32)
            found = found[:ROW_BLOCK] + found[ROW_BLOCK:]
            mask = lax.broadcasted_iota(jnp.int32, (ROW_BLOCK, per_peer), 0) == row
            reply_ref[peer] = jnp.sum(jnp.where(mask, found, 0.0), 0, keepdims=True)
        return carry

    lax.fori_loop(0, peers // UNROLL, answer, 0)
    leave.wait()


def swaps():
    count_x, count_y = lax.axis_size("bx"), lax.axis_size("by")

    def pairs(partner):
        return [
            (x * count_y + y, px * count_y + py)
            for x in range(count_x)
            for y in range(count_y)
            for px, py in [partner(x, y)]
        ]

    odd = lambda i: i + 1 if i % 2 else i - 1
    return (
        pairs(lambda x, y: (x ^ 1, y)),
        pairs(lambda x, y: (odd(x) % count_x, y)),
        pairs(lambda x, y: (x, y ^ 1)),
        pairs(lambda x, y: (x, odd(y)) if 0 < y < count_y - 1 else (x ^ 1, y)),
    )


def exchange(row_even, row_odd, packed):
    even_x, odd_x, even_y, odd_y = swaps()
    axes = ("bx", "by")

    def send(message, pairs):
        return lax.ppermute(message, axes, pairs)

    return (
        row_even,
        row_odd,
        send(row_even, even_x),
        send(row_odd, odd_x),
        packed,
        send(packed, even_y),
        send(packed, odd_y),
    )


def call(kernel, ins, outs, scratch, limit=20, flops=0):
    return pl.pallas_call(
        kernel,
        in_specs=[pl.BlockSpec(memory_space=m) for m in ins],
        out_specs=[pl.BlockSpec(memory_space=m) for _, _, m in outs],
        out_shape=[HBM(s, t) if m is HBM else jax.ShapeDtypeStruct(s, t) for s, t, m in outs],
        scratch_shapes=scratch,
        cost_estimate=pl.CostEstimate(flops=flops, bytes_accessed=flops, transcendentals=0),
        compiler_params=pltpu.CompilerParams(vmem_limit_bytes=limit * MIB),
    )


def in_hbm(*arrays):
    return [pltpu.with_memory_space_constraint(a, HBM) for a in arrays]


def prepare(root_fraction, transpiration, infiltration, clump_cell, peers, per_peer):
    roots, slot_count = root_fraction.shape
    line = (1, slot_count)
    return pl.pallas_call(
        prepare_kernel,
        in_specs=[pl.BlockSpec(memory_space=HBM)] * 4,
        out_specs=pl.BlockSpec(memory_space=HBM),
        out_shape=HBM((peers, roots + 2, per_peer), F32),
        scratch_shapes=[
            VMEM(root_fraction.shape, F32), VMEM(line, F32), VMEM(line, F32),
            VMEM(line, jnp.int32), VMEM((peers, roots + 2, per_peer), F32),
            pltpu.SemaphoreType.DMA((2 * prepare_steps(peers) + 3,)),
        ],
        name="prepare",
        compiler_params=pltpu.CompilerParams(vmem_limit_bytes=6 * MIB),
    )(*in_hbm(root_fraction, transpiration[None], infiltration[None], clump_cell[None]))


def on_device(
    h_old,
    soil_type,
    ks_scale,
    soil_table,
    clump_brick,
    clump_cell,
    root_fraction,
    transpiration,
    infiltration,
):
    layers, rows, width = h_old.shape
    peers = lax.axis_size("bx") * lax.axis_size("by")
    roots, slot_count = root_fraction.shape
    per_peer = slot_count // peers
    cells = (layers, rows, width)
    lane_msg = (rows, width)
    axes = ("bx", "by")
    on_chip = lambda *shapes: [(s, F32, VMEM) for s in shapes]
    in_main = lambda *shapes: [(s, F32, HBM) for s in shapes]
    buffers = lambda n: [VMEM(cells, F32)] * n
    semaphores = pltpu.SemaphoreType.DMA
    chunks = len(layer_chunks(layers))

    slots = lax.all_to_all(
        prepare(root_fraction, transpiration, infiltration, clump_cell, peers, per_peer),
        axes,
        split_axis=0,
        concat_axis=0,
        tiled=True,
    )
    table = jnp.pad(soil_table, ((0, 0), (0, width - soil_table.shape[1])))
    raw_msg = (3, layers, width)
    head, soil, scale, row_even, row_odd, packed = call(
        edges_kernel,
        [HBM] * 3,
        on_chip(cells) + [(cells, jnp.int32, VMEM)] + on_chip(cells, raw_msg, raw_msg, lane_msg),
        [semaphores((3 * chunks,))],
    )(*in_hbm(h_old, soil_type, ks_scale))
    pads = [VMEM((layers, rows + 2 * PAD, width), F32)] * 2
    halo = [VMEM((2,) + lane_msg, F32)]
    arrived = exchange(row_even, row_odd, packed)
    alpha, n1, half_m, ksat, room, old_sat, stored, conduct, storage = call(
        first_kernel,
        [VMEM] * 4,
        in_main(*[cells] * 7) + on_chip(*[cells] * 2),
        buffers(6) + [semaphores((7 * chunks,))],
        flops=8_000_000,
    )(head, soil, scale, table)
    own_even, own_odd, row_even, row_odd, own, lane_even, lane_odd = arrived
    residual, diagonal, vert, row_par = call(
        balance_kernel,
        [VMEM] * 8,
        on_chip(*[cells] * 3, (2, 4, layers, width)),
        pads,
        flops=4_000_000,
    )(head, conduct, storage, table, own_even, own_odd, row_even, row_odd)
    values = roots + 1
    columns = rows // ROW_BLOCK * width
    group = GROUP if peers % (2 * GROUP) == 0 else 1
    lefts = [VMEM((2 * values * ROW_BLOCK, group * per_peer), BF16)] * 2
    hots = [VMEM((columns, group * per_peer), BF16)] * 2
    row_msg = (1, layers, width)
    (
        head, sink, infil, row_even, row_odd, packed,
        alpha, n1, half_m, ksat, room, old_sat, lane_par,
    ) = call(
        middle_kernel,
        [VMEM] + [HBM] * 8 + [VMEM] * 7,
        on_chip(cells, (roots, rows, width), lane_msg, row_msg, row_msg, lane_msg)
        + on_chip(*[cells] * 6, (4,) + lane_msg),
        [VMEM((2 * values * ROW_BLOCK, columns), F32)] + lefts + hots
        + buffers(3) + halo + [semaphores((8,))],
    )(
        slots, *in_hbm(h_old, stored, alpha, n1, half_m, ksat, room, old_sat),
        residual, diagonal, vert, table, own, lane_even, lane_odd,
    )
    arrived = exchange(row_even, row_odd, packed)
    conduct, residual, diagonal, vert, denom = call(
        close_kernel,
        [VMEM] * 9,
        on_chip(*[cells] * 4, lane_msg),
        pads + buffers(2),
        limit=8,
        flops=8_000_000,
    )(head, sink, infil, alpha, n1, half_m, ksat, room, old_sat)
    head, reply = call(
        last_kernel,
        [VMEM] * 20,
        in_main(cells) + on_chip((peers, 1, per_peer)),
        buffers(3) + halo
        + [VMEM((2, 2, layers, width), F32), VMEM(lane_msg, F32), semaphores((1,))],
    )(
        slots, head, conduct, residual, diagonal, vert, denom, sink, alpha, n1, half_m,
        row_par, lane_par, *arrived,
    )
    stress = lax.all_to_all(reply, axes, split_axis=0, concat_axis=0, tiled=True)
    return head, stress.reshape(slot_count)


def solution(mesh):
    placed = (
        P(None, "bx", "by"),
        P(None, "bx", "by"),
        P(None, "bx", "by"),
        P(),
        P(("bx", "by")),
        P(("bx", "by")),
        P(None, ("bx", "by")),
        P(("bx", "by")),
        P(("bx", "by")),
    )
    return jax.shard_map(
        on_device,
        mesh=mesh,
        in_specs=placed,
        out_specs=(P(None, "bx", "by"), P(("bx", "by"))),
        check_vma=False,
    )
```

```python
import jax
import jax.numpy as jnp
from jax import lax
from jax.experimental import pallas as pl
from jax.experimental.pallas import tpu as pltpu
from jax.sharding import PartitionSpec as P


RESIDUAL_WATER = 0.05
STORAGE = 0.2
TIME_STEP = 0.5
LATERAL = 0.5
TINY = 1e-30
ROW_BLOCK = 32
HALF = 32
LAST = 64
UNROLL = 16
GROUP = 4
LOG2E = 1.4426950408889634
PAD = 8
F32 = jnp.float32
BF16 = jnp.bfloat16
MIB = 1 << 20
VMEM = pltpu.VMEM
HBM = pltpu.HBM


def lane_tables(table, shape):
    t0, t1, t2, t3 = (table[i : i + 1, :] for i in range(4))
    alpha = 4.0 * t0
    n1 = 0.2 + 2.0 * t1
    half_m = 0.5 * n1 / (1.0 + n1)
    ks3 = (0.5 * LATERAL * 3.0) * t2
    room = ((0.3 - RESIDUAL_WATER) + 0.3 * t3) * (1.0 / TIME_STEP)
    rows = (alpha, LOG2E * n1, -LOG2E * half_m, ks3, room)
    return [jnp.broadcast_to(r, shape) for r in rows]


def powers(head, alpha, n1, half_m):
    suction = jnp.maximum(alpha * jnp.maximum(-head, 0.0), TINY)
    power = jnp.exp2(n1 * lax.log(suction))
    log_base = lax.log(1.0 + suction * power)
    return power, log_base, half_m * log_base


def closure(head, alpha, n1, half_m, ksat, room):
    power, log_base, half = powers(head, alpha, n1, half_m)
    root = jnp.exp2(half)
    saturation = root * root
    share = power * saturation
    inner = 1.0 - share
    conduct = (ksat * root) * (inner * inner)
    cap = (room * (1.0 / LOG2E)) * (n1 * alpha)
    storage = STORAGE / TIME_STEP + cap * (share * jnp.exp2(-LOG2E * log_base))
    return saturation, conduct, storage


def lane_lookup(row, index):
    return jnp.take_along_axis(row, index, axis=1, mode="promise_in_bounds")


def conductivity(head, alpha, n1, half_m, ksat):
    power, _, half = powers(head, alpha, n1, half_m)
    root = jnp.exp2(half)
    inner = 1.0 - power * (root * root)
    return (ksat * root) * (inner * inner)


def edge_lanes(values, k, layers, lanes, packed):
    for part, value in enumerate(values):
        at = 2 * (part * layers + k)
        moved = pltpu.roll(value, at + 1, 1)
        packed = jnp.where((lanes == at) | (lanes == at + 1), moved, packed)
    return packed


def edge_rows(refs, row_even_ref, row_odd_ref):
    even = lax.rem(lax.axis_index("bx"), 2) == 0
    for part, ref in enumerate(refs):
        rows = ref.shape[1]
        low = ref[:, 0, :].astype(F32)
        high = ref[:, rows - 1, :].astype(F32)
        row_even_ref[part] = jnp.where(even, high, low)
        row_odd_ref[part] = jnp.where(even, low, high)


def row_halo(own_even, own_odd, row_even, row_odd):
    index = lax.axis_index("bx")
    even = lax.rem(index, 2) == 0
    low = jnp.where(even, row_odd, row_even)
    high = jnp.where(even, row_even, row_odd)
    own_low = jnp.where(even, own_odd, own_even)
    own_high = jnp.where(even, own_even, own_odd)
    low = jnp.where(index == 0, own_low, low)
    high = jnp.where(index == lax.axis_size("bx") - 1, own_high, high)
    return low, high


def lane_halo(own, lane_even, lane_odd):
    index = lax.axis_index("by")
    even = lax.rem(index, 2) == 0
    width = own.shape[1]
    lanes = lax.broadcasted_iota(jnp.int32, own.shape, 1)
    low = jnp.where(even, lane_odd, lane_even)
    high = jnp.where(even, lane_even, lane_odd)
    low = jnp.where(index == 0, pltpu.roll(own, width - 1, 1), low)
    high = jnp.where(index == lax.axis_size("by") - 1, pltpu.roll(own, 1, 1), high)
    return jnp.where(lax.rem(lanes, 2) == 0, low, pltpu.roll(high, width - 2, 1))


def edge_signs(shape):
    x, y = lax.axis_index("bx"), lax.axis_index("by")
    minus = lambda at_edge: jnp.where(at_edge, -1.0, 1.0)
    lanes = lax.broadcasted_iota(jnp.int32, shape, 1)
    return (
        minus(x == 0),
        minus(x == lax.axis_size("bx") - 1),
        jnp.where(
            lax.rem(lanes, 2) == 0, minus(y == 0), minus(y == lax.axis_size("by") - 1)
        ),
    )


def prepare_kernel(
    root_hbm, transp_hbm, infil_hbm, cell_hbm, out_hbm,
    root_ref, transp_ref, infil_ref, cell_ref, out_ref, sems,
):
    peers, fields, per_peer = out_ref.shape
    roots = fields - 2
    steps = prepare_steps(peers)
    count = peers // steps
    span = count * per_peer
    lines = [
        pltpu.make_async_copy(a, b, sems.at[2 * steps + i])
        for i, (a, b) in enumerate(
            [(transp_hbm, transp_ref), (infil_hbm, infil_ref), (cell_hbm, cell_ref)]
        )
    ]
    parts = [
        pltpu.make_async_copy(
            root_hbm.at[:, pl.ds(i * span, span)],
            root_ref.at[:, pl.ds(i * span, span)],
            sems.at[i],
        )
        for i in range(steps)
    ]
    leaves = [
        pltpu.make_async_copy(
            out_ref.at[pl.ds(i * count, count)],
            out_hbm.at[pl.ds(i * count, count)],
            sems.at[steps + i],
        )
        for i in range(steps)
    ]
    for copy in lines + parts:
        copy.start()
    for copy in lines:
        copy.wait()
    for i in range(steps):
        parts[i].wait()
        for peer in range(i * count, (i + 1) * count):
            at = slice(peer * per_peer, (peer + 1) * per_peer)
            out_ref[peer, :roots, :] = root_ref[:, at] * transp_ref[:, at]
            out_ref[peer, roots : roots + 1, :] = infil_ref[:, at]
            out_ref[peer, roots + 1 :, :] = cell_ref[:, at].astype(F32)
        leaves[i].start()
    for copy in leaves:
        copy.wait()


def prepare_steps(peers):
    return 4 if peers % 4 == 0 else 1


def layer_chunks(layers):
    size = 5 if layers % 5 == 0 else layers
    return [(at, size) for at in range(0, layers, size)]


def copies(pairs, sems, layers):
    chunks = layer_chunks(layers)
    return [
        [
            pltpu.make_async_copy(
                a.at[pl.ds(at, size)], b.at[pl.ds(at, size)], sems.at[c * len(pairs) + i]
            )
            for i, (a, b) in enumerate(pairs)
        ]
        for c, (at, size) in enumerate(chunks)
    ]


def edges_kernel(
    h_hbm, soil_hbm, ks_hbm,
    h_ref, soil_ref, ks_ref, row_even_ref, row_odd_ref, lane_ref,
    sems,
):
    layers, rows, width = h_ref.shape
    ins = copies([(h_hbm, h_ref), (soil_hbm, soil_ref), (ks_hbm, ks_ref)], sems, layers)
    for chunk in ins:
        for copy in chunk:
            copy.start()
    lanes = lax.broadcasted_iota(jnp.int32, (rows, width), 1)
    packed = jnp.zeros((rows, width), F32)
    for (at, size), arrive in zip(layer_chunks(layers), ins):
        for copy in arrive:
            copy.wait()
        for k in range(at, at + size):
            packed = edge_lanes(
                (h_ref[k], soil_ref[k].astype(F32), ks_ref[k]), k, layers, lanes, packed
            )
    lane_ref[...] = packed
    edge_rows((h_ref, soil_ref, ks_ref), row_even_ref, row_odd_ref)


def lateral_terms(k, top, size, head_pad, cond_pad, lanes):
    width = head_pad.shape[2]
    at = lambda pad, move: pad[k, PAD + top + move : PAD + top + move + size, :]
    head, conduct = at(head_pad, 0), at(cond_pad, 0)
    flow = faces = None
    for move in (-1, 1):
        both = conduct + at(cond_pad, move)
        term = both * (head - at(head_pad, move))
        flow = term if flow is None else flow + term
        faces = both if faces is None else faces + both
    for shift, edge in ((1, lanes == 0), (width - 1, lanes == width - 1)):
        both = jnp.where(edge, 0.0, conduct + pltpu.roll(conduct, shift, 1))
        flow = flow + both * (head - pltpu.roll(head, shift, 1))
        faces = faces + both
    return head, conduct, flow, faces


VERTICAL = 0.5 / (0.5 * LATERAL)


def first_kernel(
    h_ref, soil_ref, ks_ref, table_ref,
    alpha_hbm, n1_hbm, half_m_hbm, ksat_hbm, room_hbm, sat_hbm, cond_hbm, cond_ref, stor_ref,
    alpha_ref, n1_ref, half_m_ref, ksat_ref, room_ref, sat_ref, sems,
):
    layers, rows, width = h_ref.shape
    outs = copies(
        [
            (alpha_ref, alpha_hbm), (n1_ref, n1_hbm), (half_m_ref, half_m_hbm),
            (ksat_ref, ksat_hbm), (room_ref, room_hbm), (sat_ref, sat_hbm),
            (cond_ref, cond_hbm),
        ],
        sems,
        layers,
    )
    tables = lane_tables(table_ref[...], (8, width))
    for (at, size), leave in zip(layer_chunks(layers), outs):
        for k in range(at, at + size):
            for row in range(0, rows, 8):
                span = slice(row, row + 8)
                kind = soil_ref[k, span, :]
                alpha, n1, half_m, ks3, room = (lane_lookup(t, kind) for t in tables)
                ksat = ks3 * ks_ref[k, span, :]
                alpha_ref[k, span, :] = alpha
                n1_ref[k, span, :] = n1
                half_m_ref[k, span, :] = half_m
                ksat_ref[k, span, :] = ksat
                room_ref[k, span, :] = room
                saturation, conduct, storage = closure(
                    h_ref[k, span, :], alpha, n1, half_m, ksat, room
                )
                sat_ref[k, span, :] = saturation
                cond_ref[k, span, :] = conduct
                stor_ref[k, span, :] = storage
        for copy in leave:
            copy.start()
    for chunk in outs:
        for copy in chunk:
            copy.wait()


def balance_kernel(
    h_ref, cond_ref, stor_ref, table_ref,
    own_even_ref, own_odd_ref, row_even_ref, row_odd_ref,
    res_ref, diag_ref, vert_ref, row_par_ref,
    head_pad, cond_pad,
):
    _, rows, width = h_ref.shape
    head_pad[:, PAD : PAD + rows, :] = h_ref[...]
    cond_pad[:, PAD : PAD + rows, :] = cond_ref[...]
    sign_low, sign_high, _ = edge_signs((8, width))
    for side, sign in ((0, sign_low), (1, sign_high)):
        head, kind, ks = (
            row_halo(own_even_ref[i], own_odd_ref[i], row_even_ref[i], row_odd_ref[i])[side]
            for i in range(3)
        )
        pars = halo_parameters(table_ref, kind, ks, sign)
        for i in range(4):
            row_par_ref[side, i] = pars[i]
        row = PAD - 1 if side == 0 else PAD + rows
        head_pad[:, row, :] = head
        cond_pad[:, row, :] = conductivity(head, *pars)
    interior(head_pad, cond_pad, stor_ref, None, res_ref, diag_ref, vert_ref)


def interior(head_pad, cond_pad, stor_ref, source_ref, res_ref, diag_ref, vert_ref):
    layers, rows, width = res_ref.shape
    size = HALF if rows % HALF == 0 else rows
    lanes = lax.broadcasted_iota(jnp.int32, (size, width), 1)
    for top in range(0, rows, size):
        span = slice(top, top + size)
        inner = slice(PAD + top, PAD + top + size)
        vert_above = flux_above = None
        for k in range(layers):
            head, conduct, flow, faces = lateral_terms(k, top, size, head_pad, cond_pad, lanes)
            diagonal = stor_ref[k, span, :] + faces
            if k < layers - 1:
                vert = VERTICAL * (conduct + cond_pad[k + 1, inner, :])
                flux = vert * (head - head_pad[k + 1, inner, :] + 1.0)
                diagonal = diagonal + vert
                vert_ref[k, span, :] = vert
            else:
                vert = None
                flux = conduct * (2.0 * VERTICAL)
            residual = flux + flow
            if source_ref is not None:
                residual = residual + source_ref[k, span, :]
            if k:
                residual = residual - flux_above
                diagonal = diagonal + vert_above
            res_ref[k, span, :] = residual
            diag_ref[k, span, :] = diagonal
            vert_above, flux_above = vert, flux


def halo_parameters(table_ref, kind, ks, sign):
    pars = [
        lane_lookup(t, jnp.clip(kind.astype(jnp.int32), 0, kind.shape[1] - 1))
        for t in lane_tables(table_ref[...], kind.shape)[:4]
    ]
    return pars[:3] + [sign * (pars[3] * ks)]


def add_rows(array, part, row):
    pieces = [array[:row], array[row : row + 8] + part, array[row + 8 :]]
    return jnp.concatenate([p for p in pieces if p.shape[0]], 0)


def slot_places(ids, width):
    shift = width.bit_length() - 1
    row = ids >> shift
    low = ROW_BLOCK.bit_length() - 1
    return row & (ROW_BLOCK - 1), (row >> low) * width + (ids & (width - 1))


def one_hot(ids, count):
    place = lax.broadcasted_iota(jnp.int32, (count, ids.shape[1]), 0)
    return (place == ids).astype(F32).astype(BF16)


def middle_kernel(
    slots_ref, h_hbm, cond_hbm, alpha_hbm, n1_hbm, half_m_hbm, ksat_hbm, room_hbm, sat_hbm,
    res_ref, diag_ref, vert_ref, table_ref, own_ref, lane_even_ref, lane_odd_ref,
    head_ref, sink_ref, infil_ref, row_even_ref, row_odd_ref, lane_ref,
    alpha_ref, n1_ref, half_m_ref, ksat_ref, room_ref, sat_ref, lane_par_ref,
    total, left_a, left_b, hot_a, hot_b, h_ref, cond_ref, ratio_ref, halo_ref, sems,
):
    layers, rows, width = h_ref.shape
    peers, fields, per_peer = slots_ref.shape
    roots = fields - 2
    values = fields - 1
    blocks = rows // ROW_BLOCK
    half = values * ROW_BLOCK
    group = left_a.shape[1] // per_peer
    steps = peers // group
    loads = [
        pltpu.make_async_copy(a, b, sems.at[i])
        for i, (a, b) in enumerate(
            [
                (h_hbm, h_ref), (cond_hbm, cond_ref), (sat_hbm, sat_ref),
                (alpha_hbm, alpha_ref), (n1_hbm, n1_ref), (half_m_hbm, half_m_ref),
                (ksat_hbm, ksat_ref), (room_hbm, room_ref),
            ]
        )
    ]
    for copy in loads:
        copy.start()
    total[...] = jnp.zeros_like(total)

    def build(step, left, hot):
        for g in range(group):
            block = slots_ref[step * group + g]
            at = slice(g * per_peer, (g + 1) * per_peer)
            row, column = slot_places(block[values : values + 1, :].astype(jnp.int32), width)
            hot[:, at] = one_hot(column, blocks * width)
            mask = lax.broadcasted_iota(jnp.int32, (ROW_BLOCK, per_peer), 0) == row
            high = block.astype(BF16).astype(F32)
            low = block - high
            for f in range(values):
                for base, part in ((0, high), (half, low)):
                    first = base + f * ROW_BLOCK
                    left[first : first + ROW_BLOCK, at] = jnp.where(
                        mask, part[f : f + 1, :], 0.0
                    ).astype(BF16)

    def add(left, hot):
        total[...] += lax.dot_general(
            left[...], hot[...], (((1,), (1,)), ((), ())), preferred_element_type=F32
        )

    build(0, left_a, hot_a)

    def place(pair, carry):
        build(2 * pair + 1, left_b, hot_b)
        add(left_a, hot_a)
        build(jnp.minimum(2 * pair + 2, steps - 1), left_a, hot_a)
        add(left_b, hot_b)
        return carry

    lax.fori_loop(0, steps // 2, place, 0)
    for copy in loads:
        copy.wait()

    def grid(f, b):
        at = f * ROW_BLOCK
        cols = slice(b * width, (b + 1) * width)
        return total[at : at + ROW_BLOCK, cols] + total[half + at : half + at + ROW_BLOCK, cols]

    halo = lane_halo(own_ref[...], lane_even_ref[...], lane_odd_ref[...])
    pars = halo_parameters(
        table_ref,
        pltpu.roll(halo, width - 2 * layers, 1),
        pltpu.roll(halo, width - 4 * layers, 1),
        edge_signs((rows, width))[2],
    )
    for i in range(4):
        lane_par_ref[i] = pars[i]
    halo_ref[0] = halo
    halo_ref[1] = conductivity(halo, *pars)
    lanes = lax.broadcasted_iota(jnp.int32, (rows, width), 1)
    edge = (lanes == 0) | (lanes == width - 1)
    whole = lambda f: jnp.concatenate([grid(f, b) for b in range(blocks)], 0)
    infil = whole(roots)
    infil_ref[...] = infil
    value = ratio = None
    for k in range(layers):
        halo_head = pltpu.roll(halo_ref[0], (width - 2 * k) % width, 1)
        halo_cond = pltpu.roll(halo_ref[1], (width - 2 * k) % width, 1)
        both = jnp.where(edge, cond_ref[k] + halo_cond, 0.0)
        diagonal = diag_ref[k] + both
        residual = res_ref[k] + both * (h_ref[k] - halo_head)
        if k < roots:
            sink = whole(k)
            sink_ref[k] = sink
            residual = residual + sink
        if k == 0:
            target = infil - residual
        else:
            vert = vert_ref[k - 1]
            diagonal = diagonal - vert * ratio
            target = vert * value - residual
        inverse = 1.0 / diagonal
        value = target * inverse
        head_ref[k] = value
        if k < layers - 1:
            ratio = vert_ref[k] * inverse
            ratio_ref[k] = ratio
    change = value
    packed = jnp.zeros((rows, width), F32)
    for k in range(layers - 1, -1, -1):
        if k < layers - 1:
            change = head_ref[k] + ratio_ref[k] * change
        head = h_ref[k] + change
        head_ref[k] = head
        packed = edge_lanes((head,), k, layers, lanes, packed)
    lane_ref[...] = packed
    edge_rows((head_ref,), row_even_ref, row_odd_ref)


def close_kernel(
    head_ref, sink_ref, infil_ref,
    alpha_ref, n1_ref, half_m_ref, ksat_ref, room_ref, sat_ref,
    cond_ref, res_ref, diag_ref, vert_ref, denom_ref,
    head_pad, cond_pad, stor_ref, source_ref,
):
    layers, rows, _ = head_ref.shape
    roots = sink_ref.shape[0]
    denom = None
    for k in range(layers):
        room = room_ref[k]
        head = head_ref[k]
        saturation, conduct, storage = closure(
            head, alpha_ref[k], n1_ref[k], half_m_ref[k], ksat_ref[k], room
        )
        cond_ref[k] = conduct
        head_pad[k, PAD : PAD + rows, :] = head
        cond_pad[k, PAD : PAD + rows, :] = conduct
        for row, beyond in ((0, PAD - 1), (rows - 1, PAD + rows)):
            head_pad[k, beyond : beyond + 1, :] = head[row : row + 1]
            cond_pad[k, beyond : beyond + 1, :] = -conduct[row : row + 1]
        stor_ref[k] = storage
        source = room * (saturation - sat_ref[k])
        if k < roots:
            sink = sink_ref[k]
            source = source + sink
            denom = sink if denom is None else denom + sink
        if k == 0:
            source = source - infil_ref[...]
        source_ref[k] = source
    denom_ref[...] = denom
    interior(head_pad, cond_pad, stor_ref, source_ref, res_ref, diag_ref, vert_ref)


def last_kernel(
    slots_ref, old_head_ref, cond_ref, old_res_ref, old_diag_ref, vert_ref, denom_ref, sink_ref,
    alpha_ref, n1_ref, half_m_ref, row_par_ref, lane_par_ref,
    own_even_ref, own_odd_ref, row_even_ref, row_odd_ref, own_ref, lane_even_ref, lane_odd_ref,
    head_hbm, reply_ref,
    head_ref, ratio_ref, value_ref, halo_ref, side_ref, stress_ref, sems,
):
    layers, rows, width = head_ref.shape
    peers, fields, per_peer = slots_ref.shape
    roots = fields - 2
    sides = row_halo(own_even_ref[0], own_odd_ref[0], row_even_ref[0], row_odd_ref[0])
    for side in range(2):
        side_ref[side, 0] = sides[side]
        side_ref[side, 1] = conductivity(sides[side], *(row_par_ref[side, i] for i in range(4)))
    halo = lane_halo(own_ref[...], lane_even_ref[...], lane_odd_ref[...])
    halo_ref[0] = halo
    halo_ref[1] = conductivity(halo, *(lane_par_ref[i] for i in range(4)))
    size = LAST if rows % LAST == 0 else rows
    lanes = lax.broadcasted_iota(jnp.int32, (size, width), 1)
    edge = (lanes == 0) | (lanes == width - 1)
    places = lax.broadcasted_iota(jnp.int32, (8, width), 0)
    for top in range(0, rows, size):
        span = slice(top, top + size)
        value = ratio = None
        for k in range(layers):
            head, conduct = old_head_ref[k, span, :], cond_ref[k, span, :]
            halo_head = pltpu.roll(halo_ref[0, span], (width - 2 * k) % width, 1)
            halo_cond = pltpu.roll(halo_ref[1, span], (width - 2 * k) % width, 1)
            both = jnp.where(edge, conduct + halo_cond, 0.0)
            faces = both
            flow = both * (head - halo_head)
            for side, row, holds in (
                (0, 0, top == 0), (1, size - 8, top + size == rows)
            ):
                if holds:
                    part = slice(row, row + 8)
                    both = jnp.where(
                        places == (0 if side == 0 else 7),
                        conduct[part] + side_ref[side, 1, k : k + 1, :],
                        0.0,
                    )
                    more = both * (head[part] - side_ref[side, 0, k : k + 1, :])
                    faces = add_rows(faces, both, row)
                    flow = add_rows(flow, more, row)
            diagonal = old_diag_ref[k, span, :] + faces
            residual = old_res_ref[k, span, :] + flow
            if k:
                vert = vert_ref[k - 1, span, :]
                diagonal = diagonal - vert * ratio
                target = vert * value - residual
            else:
                target = -residual
            inverse = 1.0 / diagonal
            value = target * inverse
            value_ref[k, span, :] = value
            if k < layers - 1:
                ratio = vert_ref[k, span, :] * inverse
                ratio_ref[k, span, :] = ratio
        change = value
        head_ref[layers - 1, span, :] = old_head_ref[layers - 1, span, :] + change
        numer = None
        for k in range(layers - 2, -1, -1):
            change = value_ref[k, span, :] + ratio_ref[k, span, :] * change
            head = old_head_ref[k, span, :] + change
            head_ref[k, span, :] = head
            if k < roots:
                half = powers(
                    head, alpha_ref[k, span, :], n1_ref[k, span, :], half_m_ref[k, span, :]
                )[2]
                term = sink_ref[k, span, :] * jnp.exp2(half + half)
                numer = term if numer is None else numer + term
        denom = denom_ref[span, :]
        held = denom > 0.0
        stress_ref[span, :] = jnp.where(held, numer / jnp.where(held, denom, 1.0), 0.0)
    leave = pltpu.make_async_copy(head_ref, head_hbm, sems.at[0])
    leave.start()
    stress = stress_ref[...]
    high = stress.astype(BF16)
    both = jnp.concatenate([high, (stress - high.astype(F32)).astype(BF16)], 0)

    def answer(block, carry):
        for g in range(UNROLL):
            peer = block * UNROLL + g
            ids = slots_ref[peer, fields - 1 : fields, :].astype(jnp.int32)
            hot = one_hot(ids & (width - 1), width)
            found = jnp.dot(both, hot, preferred_element_type=F32)
            found = found[:rows] + found[rows:]
            place = lax.broadcasted_iota(jnp.int32, (rows, per_peer), 0)
            mask = place == (ids >> (width.bit_length() - 1))
            reply_ref[peer] = jnp.sum(jnp.where(mask, found, 0.0), 0, keepdims=True)
        return carry

    lax.fori_loop(0, peers // UNROLL, answer, 0)
    leave.wait()


def swaps():
    count_x, count_y = lax.axis_size("bx"), lax.axis_size("by")

    def pairs(partner):
        return [
            (x * count_y + y, px * count_y + py)
            for x in range(count_x)
            for y in range(count_y)
            for px, py in [partner(x, y)]
        ]

    odd = lambda i: i + 1 if i % 2 else i - 1
    return (
        pairs(lambda x, y: (x ^ 1, y)),
        pairs(lambda x, y: (odd(x) % count_x, y)),
        pairs(lambda x, y: (x, y ^ 1)),
        pairs(lambda x, y: (x, odd(y)) if 0 < y < count_y - 1 else (x ^ 1, y)),
    )


def exchange(row_even, row_odd, packed):
    even_x, odd_x, even_y, odd_y = swaps()
    axes = ("bx", "by")

    def send(message, pairs):
        return lax.ppermute(message, axes, pairs)

    return (
        row_even,
        row_odd,
        send(row_even, even_x),
        send(row_odd, odd_x),
        packed,
        send(packed, even_y),
        send(packed, odd_y),
    )


def call(kernel, ins, outs, scratch, limit=20, flops=0):
    return pl.pallas_call(
        kernel,
        in_specs=[pl.BlockSpec(memory_space=m) for m in ins],
        out_specs=[pl.BlockSpec(memory_space=m) for _, _, m in outs],
        out_shape=[HBM(s, t) if m is HBM else jax.ShapeDtypeStruct(s, t) for s, t, m in outs],
        scratch_shapes=scratch,
        cost_estimate=pl.CostEstimate(flops=flops, bytes_accessed=flops, transcendentals=0),
        compiler_params=pltpu.CompilerParams(vmem_limit_bytes=limit * MIB),
    )


def in_hbm(*arrays):
    return [pltpu.with_memory_space_constraint(a, HBM) for a in arrays]


def prepare(root_fraction, transpiration, infiltration, clump_cell, peers, per_peer):
    roots, slot_count = root_fraction.shape
    line = (1, slot_count)
    return pl.pallas_call(
        prepare_kernel,
        in_specs=[pl.BlockSpec(memory_space=HBM)] * 4,
        out_specs=pl.BlockSpec(memory_space=HBM),
        out_shape=HBM((peers, roots + 2, per_peer), F32),
        scratch_shapes=[
            VMEM(root_fraction.shape, F32), VMEM(line, F32), VMEM(line, F32),
            VMEM(line, jnp.int32), VMEM((peers, roots + 2, per_peer), F32),
            pltpu.SemaphoreType.DMA((2 * prepare_steps(peers) + 3,)),
        ],
        name="prepare",
        compiler_params=pltpu.CompilerParams(vmem_limit_bytes=6 * MIB),
    )(*in_hbm(root_fraction, transpiration[None], infiltration[None], clump_cell[None]))


def on_device(
    h_old,
    soil_type,
    ks_scale,
    soil_table,
    clump_brick,
    clump_cell,
    root_fraction,
    transpiration,
    infiltration,
):
    layers, rows, width = h_old.shape
    peers = lax.axis_size("bx") * lax.axis_size("by")
    roots, slot_count = root_fraction.shape
    per_peer = slot_count // peers
    cells = (layers, rows, width)
    lane_msg = (rows, width)
    axes = ("bx", "by")
    on_chip = lambda *shapes: [(s, F32, VMEM) for s in shapes]
    in_main = lambda *shapes: [(s, F32, HBM) for s in shapes]
    buffers = lambda n: [VMEM(cells, F32)] * n
    semaphores = pltpu.SemaphoreType.DMA
    chunks = len(layer_chunks(layers))

    slots = lax.all_to_all(
        prepare(root_fraction, transpiration, infiltration, clump_cell, peers, per_peer),
        axes,
        split_axis=0,
        concat_axis=0,
        tiled=True,
    )
    table = jnp.pad(soil_table, ((0, 0), (0, width - soil_table.shape[1])))
    raw_msg = (3, layers, width)
    head, soil, scale, row_even, row_odd, packed = call(
        edges_kernel,
        [HBM] * 3,
        on_chip(cells) + [(cells, jnp.int32, VMEM)] + on_chip(cells, raw_msg, raw_msg, lane_msg),
        [semaphores((3 * chunks,))],
    )(*in_hbm(h_old, soil_type, ks_scale))
    pads = [VMEM((layers, rows + 2 * PAD, width), F32)] * 2
    halo = [VMEM((2,) + lane_msg, F32)]
    arrived = exchange(row_even, row_odd, packed)
    alpha, n1, half_m, ksat, room, old_sat, stored, conduct, storage = call(
        first_kernel,
        [VMEM] * 4,
        in_main(*[cells] * 7) + on_chip(*[cells] * 2),
        buffers(6) + [semaphores((7 * chunks,))],
        flops=8_000_000,
    )(head, soil, scale, table)
    own_even, own_odd, row_even, row_odd, own, lane_even, lane_odd = arrived
    residual, diagonal, vert, row_par = call(
        balance_kernel,
        [VMEM] * 8,
        on_chip(*[cells] * 3, (2, 4, layers, width)),
        pads,
        flops=4_000_000,
    )(head, conduct, storage, table, own_even, own_odd, row_even, row_odd)
    values = roots + 1
    columns = rows // ROW_BLOCK * width
    group = GROUP if peers % (2 * GROUP) == 0 else 1
    lefts = [VMEM((2 * values * ROW_BLOCK, group * per_peer), BF16)] * 2
    hots = [VMEM((columns, group * per_peer), BF16)] * 2
    row_msg = (1, layers, width)
    (
        head, sink, infil, row_even, row_odd, packed,
        alpha, n1, half_m, ksat, room, old_sat, lane_par,
    ) = call(
        middle_kernel,
        [VMEM] + [HBM] * 8 + [VMEM] * 7,
        on_chip(cells, (roots, rows, width), lane_msg, row_msg, row_msg, lane_msg)
        + on_chip(*[cells] * 6, (4,) + lane_msg),
        [VMEM((2 * values * ROW_BLOCK, columns), F32)] + lefts + hots
        + buffers(3) + halo + [semaphores((8,))],
    )(
        slots, *in_hbm(h_old, stored, alpha, n1, half_m, ksat, room, old_sat),
        residual, diagonal, vert, table, own, lane_even, lane_odd,
    )
    arrived = exchange(row_even, row_odd, packed)
    conduct, residual, diagonal, vert, denom = call(
        close_kernel,
        [VMEM] * 9,
        on_chip(*[cells] * 4, lane_msg),
        pads + buffers(2),
        limit=8,
        flops=8_000_000,
    )(head, sink, infil, alpha, n1, half_m, ksat, room, old_sat)
    head, reply = call(
        last_kernel,
        [VMEM] * 20,
        in_main(cells) + on_chip((peers, 1, per_peer)),
        buffers(3) + halo
        + [VMEM((2, 2, layers, width), F32), VMEM(lane_msg, F32), semaphores((1,))],
    )(
        slots, head, conduct, residual, diagonal, vert, denom, sink, alpha, n1, half_m,
        row_par, lane_par, *arrived,
    )
    stress = lax.all_to_all(reply, axes, split_axis=0, concat_axis=0, tiled=True)
    return head, stress.reshape(slot_count)


def solution(mesh):
    placed = (
        P(None, "bx", "by"),
        P(None, "bx", "by"),
        P(None, "bx", "by"),
        P(),
        P(("bx", "by")),
        P(("bx", "by")),
        P(None, ("bx", "by")),
        P(("bx", "by")),
        P(("bx", "by")),
    )
    return jax.shard_map(
        on_device,
        mesh=mesh,
        in_specs=placed,
        out_specs=(P(None, "bx", "by"), P(("bx", "by"))),
        check_vma=False,
    )
```
